256 devices in a mesh: gx: 4 (over x), gy: 8 (over z), gz: 8 (over y, core).
Axes of the slice: x: 4, y: 4, z: 8, core: 2. Of those that a mesh axis runs over, the one named last changes fastest.
Arguments:
- orbitals: float32 [8, 64, 128, 1024], P(None, 'gx', 'gy', 'gz'), may hold values from -7 to 7
- potential: float32 [64, 128, 1024], P('gx', 'gy', 'gz'), may hold values from -2 to 1
- locked: bfloat16 [64, 64, 128, 1024], P(None, 'gx', 'gy', 'gz'), may hold values from -160 to 160
- sphere_cell: int32 [4, 8, 8, 16384], P('gx', 'gy', 'gz'), may hold values from 0 to 32767
- sphere_owner: int32 [4, 8, 8, 16384], P('gx', 'gy', 'gz'), may hold values from 0 to 26
- sphere_atom: int32 [4, 8, 8, 16384], P('gx', 'gy', 'gz'), may hold values from 0 to 31
- sphere_profile: float32 [4, 8, 8, 9, 16384], P('gx', 'gy', 'gz'), may hold values from -1.2 to 1.2
- atom_strength: float32 [4, 8, 8, 32, 9], P('gx', 'gy', 'gz'), may hold values from -0.5 to 2
- atom_channels: int32 [4, 8, 8, 32], P('gx', 'gy', 'gz'), may hold values from 0 to 9, as said below
Outputs:
- projected: float32 [8, 64, 128, 1024], P(None, 'gx', 'gy', 'gz')
The draws below stay inside these ranges and needn't reach their ends.
Inputs may be any that keep to these rules, and one draw needn't show every extreme that they name: `sphere_owner`: A code o stands for the domain (e, f, g) steps away along the three axes, o = 9 (e + 1) + 3 (f + 1) + (g + 1), with the grid's ends joined; every code occurs. `atom_channels`: each entry is 0, 1, 4 or 9; the first slot of every domain has 9.
All inputs are finite; a program needn't handle non-finite values.
Results may differ from the reference program's by a relative error of at most 0.0018.
Values sent between devices are 32-bit elements; how exact they have to be, the bound alone decides.
A program may use at most 128 MiB of HBM per device.

```python
import jax
import jax.numpy as jnp
from jax import lax

CX = 16
CY = 16
CZ = 128
ATOM_DEV = 32
POINTS = 16384
ORBS = 8
LOCKED = 64
NPROJ = 9
CELLS = 32768
NX = 64
NY = 128
NZ = 1024
N_GX = 4
N_GY = 8
N_GZ = 8


def unit_slab(key, position, slab):
    subkey = jax.random.fold_in(jax.random.fold_in(jax.random.fold_in(key, 11), position), slab)
    values = jnp.clip(jax.random.normal(subkey, (NY, NZ), jnp.float32), -5.0, 5.0)
    return values


def noise_slab(key, position, slab):
    subkey = jax.random.fold_in(jax.random.fold_in(jax.random.fold_in(key, 17), position), slab)
    values = jnp.clip(jax.random.normal(subkey, (NY, NZ), jnp.float32), -5.0, 5.0)
    return values


def slab_scale(slab):
    position_one = slab.astype(jnp.float32) / NX
    position_two = jnp.arange(NY, dtype=jnp.float32)[:, None] / NY
    position_three = jnp.arange(NZ, dtype=jnp.float32)[None, :] / NZ
    exponent = 0.6 * position_one + 0.2 * position_two + 0.2 * position_three
    return 10.0 ** exponent


def orbital_shape(slab):
    position_one = slab.astype(jnp.float32) / NX
    position_two = jnp.arange(NY, dtype=jnp.float32)[:, None] / NY
    position_three = jnp.arange(NZ, dtype=jnp.float32)[None, :] / NZ
    return 0.5 + position_one + 0.5 * position_two + 0.0 * position_three


def draw_locked(key, part):
    weights = 10.0 ** (0.5 * jax.random.uniform(jax.random.fold_in(key, 13), (LOCKED,), jnp.float32))
    offsets = jax.random.permutation(jax.random.fold_in(key, 29), LOCKED - 1)[:7].astype(jnp.int32) + 1
    blend = jax.random.uniform(jax.random.fold_in(key, 23), (LOCKED, 7), jnp.float32, -0.13, 0.13)
    rows = jnp.arange(LOCKED, dtype=jnp.int32)

    def single(slab):
        fields = lax.map(lambda position: unit_slab(key, position, slab), rows)
        total = fields + 0.4
        for member in range(7):
            partner = jnp.take(fields, (rows + offsets[member]) % LOCKED, axis=0)
            total = total + blend[:, member][:, None, None] * partner
        values = total * slab_scale(slab)[None] * weights[:, None, None]
        return jnp.clip(values, -160.0, 160.0).astype(jnp.bfloat16)
    stacked = lax.map(single, jnp.arange(NX, dtype=jnp.int32))
    return jnp.moveaxis(stacked, 0, 1)


def draw_orbitals(key, part):
    amplitude = jax.random.uniform(jax.random.fold_in(key, 37), (ORBS,), jnp.float32, 0.08, 0.16)

    def single(slab):
        shape_field = orbital_shape(slab)

        def one_orbital(position):
            values = 0.6 * unit_slab(key, position, slab) + 0.8 * noise_slab(key, position, slab)
            values = values + amplitude[position] * shape_field
            return jnp.clip(values, -7.0, 7.0)
        return lax.map(one_orbital, jnp.arange(ORBS, dtype=jnp.int32))
    stacked = lax.map(single, jnp.arange(NX, dtype=jnp.int32))
    return jnp.moveaxis(stacked, 0, 1)


def draw_sphere_profile(key, part):
    subkey = jax.random.fold_in(key, 31)
    shape = (N_GX, N_GY, N_GZ, NPROJ, POINTS)
    values = 0.2 * jnp.clip(jax.random.normal(subkey, shape, jnp.float32), -6.0, 6.0)
    channel = jnp.arange(NPROJ, dtype=jnp.int32)[None, None, None, :, None]
    return jnp.where(channel == 0, jnp.abs(values), values)


def draw_atom_channels(key, part):
    level_pick = jax.random.randint(jax.random.fold_in(key, 19), (N_GX, N_GY, N_GZ, ATOM_DEV), 0, 4)
    levels = jnp.array([0, 1, 4, 9], jnp.int32)
    counts = jnp.take(levels, level_pick)
    return counts.at[:, :, :, 0].set(9)


def touch_ends(entries, rng, smallest, high):
    dims = entries.shape
    place = [jax.random.randint(jax.random.fold_in(rng, axis), (), 0, dims[axis]) for axis in range(len(dims))]
    entries = entries.at[tuple(place)].set(smallest)
    longest = dims.index(max(dims))
    place[longest] = (place[longest] + 1) % dims[longest]
    return entries.at[tuple(place)].set(high)


def shard_levels(own_key, dims, shards, least, largest):
    level = 1.0
    for axis_at, parts in shards:
        heights = jax.random.uniform(jax.random.fold_in(jax.random.fold_in(own_key, 6), axis_at), (parts,), jnp.float32, least / len(shards), largest / len(shards))
        level = level * jnp.repeat(jnp.exp(heights), dims[axis_at] // parts).reshape((-1,) + (1,) * (len(dims) - 1 - axis_at))
    return level


def setup_inputs(seed: int = 0) -> dict:
    arg_keys = jax.random.split(jax.random.key(seed), 10)
    return {
        "orbitals": draw_orbitals(jax.random.fold_in(arg_keys[9], 71), 0),
        "potential": jnp.clip(-2.0 + 3.0 * jax.random.uniform(arg_keys[1], (NX, NY, NZ), jnp.float32) ** shard_levels(arg_keys[1], (NX, NY, NZ), ((0, 4), (1, 8), (2, 8)), -0.2, 0.2), -2.0, 1.0),
        "locked": draw_locked(jax.random.fold_in(arg_keys[9], 71), 0),
        "sphere_cell": touch_ends(jax.random.randint(arg_keys[3], (N_GX, N_GY, N_GZ, POINTS), 0, CELLS), jax.random.fold_in(arg_keys[3], 1), 0, CELLS - 1).astype(jnp.int32),
        "sphere_owner": touch_ends(jax.random.randint(arg_keys[4], (N_GX, N_GY, N_GZ, POINTS), 0, 27), jax.random.fold_in(arg_keys[4], 1), 0, 26).astype(jnp.int32),
        "sphere_atom": touch_ends(jax.random.randint(arg_keys[5], (N_GX, N_GY, N_GZ, POINTS), 0, ATOM_DEV), jax.random.fold_in(arg_keys[5], 1), 0, ATOM_DEV - 1).astype(jnp.int32),
        "sphere_profile": draw_sphere_profile(jax.random.fold_in(arg_keys[9], 71), 0),
        "atom_strength": jnp.clip(-0.5 + 2.5 * jax.random.uniform(arg_keys[7], (N_GX, N_GY, N_GZ, ATOM_DEV, NPROJ), jnp.float32) ** shard_levels(arg_keys[7], (N_GX, N_GY, N_GZ, ATOM_DEV, NPROJ), ((0, 4), (1, 8), (2, 8)), -0.2, 0.2), -0.5, 2.0),
        "atom_channels": draw_atom_channels(jax.random.fold_in(arg_keys[9], 71), 0),
    }


STENCIL_WEIGHTS = (-205.0 / 72.0, 8.0 / 5.0, -1.0 / 5.0, 8.0 / 315.0, -1.0 / 560.0)

def slot_onehot(owners, atom_ids, atom_slots):
    slot_ids = owners * atom_slots + atom_ids
    labels = jnp.arange(27 * atom_slots, dtype=jnp.int32)
    return (labels[:, None] == slot_ids[None, :]).astype(jnp.float32)

def gather_slots(flat_orbitals, cell_index, onehot, profile):
    values = jnp.take(flat_orbitals, cell_index, axis=1)
    products = (profile[:, None, :] * values[None, :, :]).reshape(-1, cell_index.shape[0])
    return lax.dot_general(onehot.astype(jnp.float32), products.astype(jnp.float32), (((1,), (1,)), ((), ())), precision=lax.Precision.HIGHEST, preferred_element_type=jnp.float32)

def spread_terms(returned, cell_index, onehot, profile, orbit_count, cell_count):
    picked = lax.dot_general(returned.astype(jnp.float32), onehot.astype(jnp.float32), (((0,), (0,)), ((), ())), precision=lax.Precision.HIGHEST, preferred_element_type=jnp.float32)
    picked = picked.reshape(profile.shape[0], orbit_count, cell_index.shape[0])
    spread = jnp.sum(profile[:, None, :] * picked, axis=0)
    return jnp.zeros((orbit_count, cell_count), jnp.float32).at[:, cell_index].add(spread)

def locked_solve(gram_matrix, correlation):
    factor = jnp.linalg.cholesky(gram_matrix)
    middle = lax.linalg.triangular_solve(factor, correlation, left_side=True, lower=True)
    return lax.linalg.triangular_solve(factor, middle, left_side=True, lower=True, transpose_a=True)

def to_blocks(grid_field):
    leading = grid_field.shape[0]
    shaped = grid_field.reshape(leading, N_GX, CX, N_GY, CY, N_GZ, CZ)
    return shaped.transpose(1, 3, 5, 0, 2, 4, 6).reshape(N_GX * N_GY * N_GZ, leading, CX * CY * CZ)

def from_blocks(blocks):
    leading = blocks.shape[1]
    shaped = blocks.reshape(N_GX, N_GY, N_GZ, leading, CX, CY, CZ)
    return shaped.transpose(3, 0, 4, 1, 5, 2, 6).reshape(leading, N_GX * CX, N_GY * CY, N_GZ * CZ)

def reference(orbitals, potential, locked, sphere_cell, sphere_owner, sphere_atom, sphere_profile, atom_strength, atom_channels):
    domains = N_GX * N_GY * N_GZ
    cell_count = CX * CY * CZ
    laplace = 3.0 * STENCIL_WEIGHTS[0] * orbitals
    for dimension in (1, 2, 3):
        for distance in range(1, 5):
            laplace = laplace + STENCIL_WEIGHTS[distance] * (jnp.roll(orbitals, distance, dimension) + jnp.roll(orbitals, -distance, dimension))
    local_part = -0.5 * laplace + potential[None] * orbitals
    cells_flat = sphere_cell.reshape(domains, POINTS)
    owners_flat = sphere_owner.reshape(domains, POINTS)
    atoms_flat = sphere_atom.reshape(domains, POINTS)
    profile_flat = sphere_profile.reshape(domains, NPROJ, POINTS)

    def partial_sums(inputs):
        flat_orbitals, cell_index, owners, atom_ids, profile = inputs
        onehot = slot_onehot(owners, atom_ids, ATOM_DEV)
        return gather_slots(flat_orbitals, cell_index, onehot, profile)
    slot_sums = lax.map(partial_sums, (to_blocks(orbitals), cells_flat, owners_flat, atoms_flat, profile_flat))
    slot_sums = slot_sums.reshape(N_GX, N_GY, N_GZ, 3, 3, 3, ATOM_DEV * NPROJ * ORBS)
    coefficient = jnp.zeros((N_GX, N_GY, N_GZ, ATOM_DEV * NPROJ * ORBS), jnp.float32)
    for neighbour in range(27):
        step_one = neighbour // 9 - 1
        step_two = neighbour // 3 % 3 - 1
        step_three = neighbour % 3 - 1
        coefficient = coefficient + jnp.roll(slot_sums[:, :, :, step_one + 1, step_two + 1, step_three + 1], (step_one, step_two, step_three), (0, 1, 2))
    active = jnp.arange(NPROJ, dtype=jnp.int32)[None, None, None, None, :] < atom_channels[..., None]
    strength = jnp.where(active, atom_strength, 0.0)
    weighted = coefficient.reshape(N_GX, N_GY, N_GZ, ATOM_DEV, NPROJ, ORBS) * strength[..., None]
    weighted = weighted.reshape(N_GX, N_GY, N_GZ, ATOM_DEV * NPROJ * ORBS)
    shifted = []
    for neighbour in range(27):
        step_one = neighbour // 9 - 1
        step_two = neighbour // 3 % 3 - 1
        step_three = neighbour % 3 - 1
        shifted.append(jnp.roll(weighted, (-step_one, -step_two, -step_three), (0, 1, 2)))
    returned = jnp.stack(shifted, axis=3).reshape(domains, 27 * ATOM_DEV, NPROJ * ORBS)

    def spread(inputs):
        back, cell_index, owners, atom_ids, profile = inputs
        onehot = slot_onehot(owners, atom_ids, ATOM_DEV)
        return spread_terms(back, cell_index, onehot, profile, ORBS, cell_count)
    nonlocal_blocks = lax.map(spread, (returned, cells_flat, owners_flat, atoms_flat, profile_flat))
    applied = local_part + from_blocks(nonlocal_blocks)
    rounded = applied.astype(jnp.bfloat16)

    def accumulate(running, position):
        gram_matrix, correlation = running
        locked_slab = lax.dynamic_slice_in_dim(locked, position, 1, 1).reshape(LOCKED, NY * NZ).astype(jnp.float32)
        applied_slab = lax.dynamic_slice_in_dim(rounded, position, 1, 1).reshape(ORBS, NY * NZ).astype(jnp.float32)
        gram_matrix = gram_matrix + lax.dot_general(locked_slab.astype(jnp.float32), locked_slab.astype(jnp.float32), (((1,), (1,)), ((), ())), precision=lax.Precision.HIGHEST, preferred_element_type=jnp.float32)
        correlation = correlation + lax.dot_general(locked_slab.astype(jnp.float32), applied_slab.astype(jnp.float32), (((1,), (1,)), ((), ())), precision=lax.Precision.HIGHEST, preferred_element_type=jnp.float32)
        return ((gram_matrix, correlation), None)
    start = (jnp.zeros((LOCKED, LOCKED), jnp.float32), jnp.zeros((LOCKED, ORBS), jnp.float32))
    (gram_matrix, correlation), unused = lax.scan(accumulate, start, jnp.arange(NX, dtype=jnp.int32))
    mixing = locked_solve(gram_matrix, correlation).astype(jnp.bfloat16)

    def correct(position):
        locked_slab = lax.dynamic_slice_in_dim(locked, position, 1, 1).reshape(LOCKED, NY * NZ)
        return lax.dot_general(mixing.astype(jnp.float32), locked_slab.astype(jnp.float32), (((0,), (0,)), ((), ())), preferred_element_type=jnp.float32)
    corrections = lax.map(correct, jnp.arange(NX, dtype=jnp.int32))
    correction = jnp.moveaxis(corrections, 0, 1).reshape(ORBS, NX, NY, NZ)
    return applied - correction
```

```python
import jax
import jax.numpy as jnp
import numpy as np
from jax import lax
from jax.experimental import pallas as pl
from jax.experimental.pallas import tpu as pltpu
from jax.sharding import PartitionSpec as P

STENCIL_WEIGHTS = (-205.0 / 72.0, 8.0 / 5.0, -1.0 / 5.0, 8.0 / 315.0, -1.0 / 560.0)
MESH = pl.DeviceIdType.MESH
F32 = jnp.float32
BF16 = jnp.bfloat16
HIGHEST = lax.Precision.HIGHEST

ORBS = 8
ROWS = 256
LANES = 128
SLOTS = 32
OWNERS = 32
CHANNELS = 9
POINTS = 16384
LOCKED = 64
CHUNK = 1024
STEPS = POINTS // CHUNK
RH = 64
NB = ROWS // RH
PAIR = CHANNELS * OWNERS
NS = ORBS * SLOTS

NT = (((1,), (1,)), ((), ()))
TN = (((0,), (0,)), ((), ()))


def onehot(count, index):
    ids = lax.broadcasted_iota(jnp.int32, (count, index.shape[1]), 0)
    return jnp.where(ids == index, 1.0, 0.0).astype(BF16)


def cell_parts(cell):
    line = cell >> 7
    return cell & (LANES - 1), line & (RH - 1), line // RH


def cell_onehot(lane, block):
    lanes = onehot(LANES, lane)
    blocks = onehot(16, block)
    return jnp.concatenate([lanes * blocks[b : b + 1] for b in range(NB)], axis=0)


def split(value):
    high = value.astype(BF16)
    return high, (value - high.astype(F32)).astype(BF16)


def spread_rows(rows, mask):
    return jnp.concatenate([mask * rows[i : i + 1] for i in range(rows.shape[0])], axis=0)


def picked_rows(values, hit, count, height):
    parts = [
        jnp.sum(jnp.where(hit, values[n * height : (n + 1) * height], 0.0), axis=0, keepdims=True)
        for n in range(count)
    ]
    return jnp.concatenate(parts, axis=0)


def gather_body(
    orb, cell, owner, atom, prof, locked, strength, chans, rep, pick,
    sums, gram, lines, yface, zface, spread_strength,
    table, acc, wide, gacc,
):
    step = pl.program_id(0)

    @pl.when(step == 0)
    def _():
        for n in range(ORBS):
            for b in range(NB):
                table[n * RH : (n + 1) * RH, b * LANES : (b + 1) * LANES] = orb[
                    n, b * RH : (b + 1) * RH, :
                ].astype(BF16)
        acc[...] = jnp.zeros_like(acc)
        gacc[...] = jnp.zeros_like(gacc)
        whole = orb[...].reshape(ORBS * 16, 16, LANES)
        yface[0] = whole[:, 0:4, :]
        yface[1] = whole[:, 12:16, :]
        ends = lax.dot_general(
            pick[...], orb[...].reshape(ORBS * ROWS, LANES), NT,
            precision=HIGHEST, preferred_element_type=F32,
        )
        zface[0] = ends[0:4]
        zface[1] = ends[4:8]
        grown = lax.dot_general(
            strength[...], rep[...], TN, precision=HIGHEST, preferred_element_type=F32
        )
        limit = jnp.dot(
            chans[...].astype(F32), rep[...], precision=HIGHEST, preferred_element_type=F32
        )
        channel = lax.broadcasted_iota(jnp.int32, (CHANNELS, NS), 0).astype(F32)
        spread_strength[...] = jnp.where(channel < limit - 0.5, grown, 0.0)

    lane, low, block = cell_parts(cell[...])
    hot = cell_onehot(lane, block)
    found = jnp.dot(table[...], hot, preferred_element_type=F32)
    hit = lax.broadcasted_iota(jnp.int32, (RH, CHUNK), 0) == low
    values = picked_rows(found, hit, ORBS, RH).astype(BF16)
    right = spread_rows(values, onehot(SLOTS, atom[...]))
    owners = onehot(OWNERS, owner[...])
    high, rest = split(prof[...])
    left = jnp.concatenate([spread_rows(high, owners), spread_rows(rest, owners)], axis=0)
    acc[...] += lax.dot_general(left, right, NT, preferred_element_type=F32)

    wide[...] = locked[...].astype(F32).reshape(LOCKED * 16, LANES)
    rows = [wide[pl.ds(r, LOCKED, stride=16), :].astype(BF16) for r in range(16)]
    for r in range(16):
        lines[r] = rows[r]
    flat = jnp.concatenate(rows, axis=1)
    gacc[...] += lax.dot_general(flat, flat, NT, preferred_element_type=F32)

    @pl.when(step == STEPS - 1)
    def _():
        for p in range(CHANNELS):
            sums[:, p, :] = (
                acc[p * OWNERS : (p + 1) * OWNERS, :]
                + acc[PAIR + p * OWNERS : PAIR + (p + 1) * OWNERS, :]
            )
        gram[:, 0:64] = gacc[0:32, :]
        gram[:, 64:128] = gacc[32:64, :]


def point_specs():
    return [
        pl.BlockSpec((1, CHUNK), lambda i: (0, i)),
        pl.BlockSpec((1, CHUNK), lambda i: (0, i)),
        pl.BlockSpec((1, CHUNK), lambda i: (0, i)),
        pl.BlockSpec((CHANNELS, CHUNK), lambda i: (0, i)),
    ]


def fixed(*shape):
    return pl.BlockSpec(shape, lambda i: (0,) * len(shape))


def gather(orb, cell, owner, atom, prof, locked, strength, chans):
    rep = np.zeros((SLOTS, NS), np.float32)
    for n in range(ORBS):
        rep[np.arange(SLOTS), n * SLOTS + np.arange(SLOTS)] = 1.0
    pick = np.zeros((8, LANES), np.float32)
    for j in range(4):
        pick[j, j] = 1.0
        pick[4 + j, LANES - 4 + j] = 1.0
    return pl.pallas_call(
        gather_body,
        grid=(STEPS,),
        in_specs=[fixed(ORBS, ROWS, LANES)]
        + point_specs()
        + [
            pl.BlockSpec((LOCKED, 16, LANES), lambda i: (0, i, 0)),
            fixed(SLOTS, CHANNELS),
            fixed(1, SLOTS),
            fixed(SLOTS, NS),
            fixed(8, LANES),
        ],
        out_specs=[
            fixed(OWNERS, CHANNELS, NS),
            fixed(32, 128),
            pl.BlockSpec((16, LOCKED, LANES), lambda i: (i, 0, 0)),
            fixed(2, ORBS * 16, 4, LANES),
            fixed(2, 4, ORBS * ROWS),
            fixed(CHANNELS, NS),
        ],
        out_shape=[
            jax.ShapeDtypeStruct((OWNERS, CHANNELS, NS), F32),
            jax.ShapeDtypeStruct((32, 128), F32),
            jax.ShapeDtypeStruct((ROWS, LOCKED, LANES), BF16),
            jax.ShapeDtypeStruct((2, ORBS * 16, 4, LANES), F32),
            jax.ShapeDtypeStruct((2, 4, ORBS * ROWS), F32),
            jax.ShapeDtypeStruct((CHANNELS, NS), F32),
        ],
        scratch_shapes=[
            pltpu.VMEM((ORBS * RH, NB * LANES), BF16),
            pltpu.VMEM((2 * PAIR, NS), F32),
            pltpu.VMEM((LOCKED * 16, LANES), F32),
            pltpu.VMEM((LOCKED, LOCKED), F32),
        ],
        compiler_params=pltpu.CompilerParams(vmem_limit_bytes=40 << 20),
        name="gather_sums",
    )(orb, cell, owner, atom, prof, locked, strength, chans, rep, pick)


def offset_of(code):
    return code // 9 - 1, code // 3 % 3 - 1, code % 3 - 1


CODES = [code for code in range(27) if code != 13]


def device(shift):
    spot = []
    for name, move in zip(("gx", "gy", "gz"), shift):
        size = lax.axis_size(name)
        spot.append(lax.rem(lax.axis_index(name) + (move + size), size))
    return tuple(spot)


def axis_partners():
    found = []
    for axis, name in ((2, "gz"), (1, "gy"), (0, "gx")):
        group = []
        for k in range(1, lax.axis_size(name)):
            shift = [0, 0, 0]
            shift[axis] = k
            group.append(tuple(shift))
        found.append(group)
    return found


def canonical(shift):
    sizes = [lax.axis_size(name) for name in ("gx", "gy", "gz")]
    return tuple(move % size for move, size in zip(shift, sizes))


def meet(shifts):
    barrier = pltpu.get_barrier_semaphore()
    for shift in shifts:
        pl.semaphore_signal(barrier, inc=1, device_id=device(shift), device_id_type=MESH)
    pl.semaphore_wait(barrier, len(shifts))


def remote(source, target, send, receive, shift):
    return pltpu.make_async_remote_copy(
        src_ref=source, dst_ref=target, send_sem=send, recv_sem=receive,
        device_id=device(shift), device_id_type=MESH,
    )


def reduce_start(source, slots, send, receive, base, group):
    copies = [
        remote(source, slots.at[base + k], send.at[base + k], receive.at[base + k], shift)
        for k, shift in enumerate(group)
    ]
    for copy in copies:
        copy.start()
    return copies


def reduce_finish(own, slots, base, copies):
    total = own
    for k, copy in enumerate(copies):
        copy.wait_recv()
        total = total + slots[base + k]
    return total


def exchange_body(
    sums, gram, strength, orb, yface, zface,
    returned, xhalo, yhalo, zhalo, inverse,
    landed, weighted, stage, slots,
    send1, recv1, send2, recv2, sendg, recvg, sendh, recvh,
):
    groups = axis_partners()
    everyone = {canonical(offset_of(code)) for code in CODES}
    for group in groups:
        everyone |= {canonical(shift) for shift in group}
    meet(sorted(everyone))

    first = [
        remote(sums.at[c], landed.at[c], send1.at[c], recv1.at[c], offset_of(c)) for c in CODES
    ]
    for copy in first:
        copy.start()
    sent = reduce_start(gram, slots, sendg, recvg, 0, groups[0])
    halos = [
        remote(orb.at[:, pl.ds(192, 64), :], xhalo.at[0], sendh.at[0], recvh.at[0], (1, 0, 0)),
        remote(orb.at[:, pl.ds(0, 64), :], xhalo.at[1], sendh.at[1], recvh.at[1], (-1, 0, 0)),
        remote(yface.at[1], yhalo.at[0], sendh.at[2], recvh.at[2], (0, 1, 0)),
        remote(yface.at[0], yhalo.at[1], sendh.at[3], recvh.at[3], (0, -1, 0)),
        remote(zface.at[1], zhalo.at[0], sendh.at[4], recvh.at[4], (0, 0, 1)),
        remote(zface.at[0], zhalo.at[1], sendh.at[5], recvh.at[5], (0, 0, -1)),
    ]
    for copy in halos:
        copy.start()
    everything = first + sent + halos

    total = sums[13]
    for code, copy in zip(CODES, first):
        copy.wait_recv()
        total = total + landed[code]
    weighted[...] = total * strength[...]
    second = []
    for code in CODES:
        back = tuple(-move for move in offset_of(code))
        copy = remote(weighted, returned.at[code], send2.at[code], recv2.at[code], back)
        copy.start()
        second.append(copy)
    returned[13] = weighted[...]
    everything += second

    matrix = gram[...]
    base = 0
    for level, group in enumerate(groups):
        matrix = reduce_finish(matrix, slots, base, sent)
        base += len(group)
        if level < 2:
            stage[level] = matrix
            sent = reduce_start(stage.at[level], slots, sendg, recvg, base, groups[level + 1])
            everything += sent
    inverse[...] = matrix
    for copy in second + halos:
        copy.wait_recv()
    for copy in everything:
        copy.wait_send()


def vmem():
    return pl.BlockSpec(memory_space=pltpu.VMEM)


def anywhere():
    return pl.BlockSpec(memory_space=pl.ANY)


def exchange(sums, gram, strength, orb, yface, zface):
    dma = pltpu.SemaphoreType.DMA
    return pl.pallas_call(
        exchange_body,
        in_specs=[vmem(), vmem(), vmem(), anywhere(), anywhere(), anywhere()],
        out_specs=[vmem(), anywhere(), anywhere(), anywhere(), vmem()],
        out_shape=[
            jax.ShapeDtypeStruct((OWNERS, CHANNELS, NS), F32),
            jax.ShapeDtypeStruct((2, ORBS, 64, LANES), F32),
            jax.ShapeDtypeStruct((2, ORBS * 16, 4, LANES), F32),
            jax.ShapeDtypeStruct((2, 4, ORBS * ROWS), F32),
            jax.ShapeDtypeStruct((32, 128), F32),
        ],
        scratch_shapes=[
            pltpu.VMEM((27, CHANNELS, NS), F32),
            pltpu.VMEM((CHANNELS, NS), F32),
            pltpu.VMEM((2, 32, 128), F32),
            pltpu.VMEM((17, 32, 128), F32),
            dma((27,)), dma((27,)), dma((27,)), dma((27,)),
            dma((17,)), dma((17,)), dma((6,)), dma((6,)),
        ],
        compiler_params=pltpu.CompilerParams(collective_id=0, has_side_effects=True),
        name="exchange",
    )(sums, gram, strength, orb, yface, zface)


def stencil_matrices():
    inner = np.zeros((LANES, LANES), np.float64)
    outer = np.zeros((8, LANES), np.float64)
    for lane in range(LANES):
        inner[lane, lane] = -1.5 * STENCIL_WEIGHTS[0]
        for k in range(1, 5):
            weight = -0.5 * STENCIL_WEIGHTS[k]
            for spot in (lane - k, lane + k):
                if spot < 0:
                    outer[spot + 4, lane] = weight
                elif spot >= LANES:
                    outer[4 + spot - LANES, lane] = weight
                else:
                    inner[spot, lane] = weight
    return inner.astype(np.float32), outer.astype(np.float32)


def apply_body(
    orb, cell, owner, atom, prof, returned, xhalo, yhalo, zhalo, potential, lines, inner, outer,
    applied, partial,
    acc, back, local, tall, ends,
):
    step = pl.program_id(0)

    @pl.when(step == 0)
    def _():
        acc[...] = jnp.zeros_like(acc)
        code = lax.broadcasted_iota(jnp.int32, (OWNERS, NS), 0)
        stacked = [jnp.where(code < 27, returned[:, p, :], 0.0) for p in range(CHANNELS)]
        high, rest = split(jnp.concatenate(stacked, axis=0).T)
        back[...] = jnp.concatenate([high, rest, high], axis=1)
        ends[0:4] = zhalo[0]
        ends[4:8] = zhalo[1]
        for n in range(ORBS):
            centre = orb[n]
            total = jnp.dot(centre, inner[...], precision=HIGHEST, preferred_element_type=F32)
            total += lax.dot_general(
                ends[:, n * ROWS : (n + 1) * ROWS], outer[...], TN,
                precision=HIGHEST, preferred_element_type=F32,
            )
            total += potential[...] * centre
            long = jnp.concatenate([xhalo[0, n], centre, xhalo[1, n]], axis=0)
            tall[:, 0:4, :] = yhalo[0, n * 16 : (n + 1) * 16]
            tall[:, 4:20, :] = centre.reshape(16, 16, LANES)
            tall[:, 20:24, :] = yhalo[1, n * 16 : (n + 1) * 16]
            for k in range(1, 5):
                pair = long[64 - 16 * k : 320 - 16 * k] + long[64 + 16 * k : 320 + 16 * k]
                side = tall[:, 4 - k : 20 - k, :] + tall[:, 4 + k : 20 + k, :]
                total += (-0.5 * STENCIL_WEIGHTS[k]) * (pair + side.reshape(ROWS, LANES))
            local[n] = total

    lane, low, block = cell_parts(cell[...])
    hot = cell_onehot(lane, block)
    owners = onehot(OWNERS, owner[...])
    high, rest = split(prof[...])
    left = spread_rows(high, owners)
    left = jnp.concatenate([left, left, spread_rows(rest, owners)], axis=0)
    near = jnp.dot(back[...], left, preferred_element_type=F32)
    hit = lax.broadcasted_iota(jnp.int32, (SLOTS, CHUNK), 0) == atom[...]
    terms = picked_rows(near, hit, ORBS, SLOTS).astype(BF16)
    acc[...] += lax.dot_general(
        spread_rows(terms, onehot(RH, low)), hot, NT, preferred_element_type=F32
    )

    @pl.when(step == STEPS - 1)
    def _():
        for n in range(ORBS):
            for b in range(NB):
                applied[b * RH : (b + 1) * RH, n, :] = (
                    local[n, b * RH : (b + 1) * RH, :]
                    + acc[n * RH : (n + 1) * RH, b * LANES : (b + 1) * LANES]
                )
        total = jnp.zeros((ORBS, LOCKED), F32)
        for g in range(ROWS // 16):
            mine = jnp.concatenate([applied[g * 16 + r].astype(BF16) for r in range(16)], axis=1)
            kept = jnp.concatenate([lines[g * 16 + r] for r in range(16)], axis=1)
            total += lax.dot_general(mine, kept, NT, preferred_element_type=F32)
        partial[:, 0:LOCKED] = total
        partial[:, LOCKED:128] = jnp.zeros((ORBS, 128 - LOCKED), F32)


def apply(orb, cell, owner, atom, prof, returned, xhalo, yhalo, zhalo, potential, lines):
    inner, outer = stencil_matrices()
    return pl.pallas_call(
        apply_body,
        grid=(STEPS,),
        in_specs=[fixed(ORBS, ROWS, LANES)]
        + point_specs()
        + [
            fixed(OWNERS, CHANNELS, NS),
            fixed(2, ORBS, 64, LANES),
            fixed(2, ORBS * 16, 4, LANES),
            fixed(2, 4, ORBS * ROWS),
            fixed(ROWS, LANES),
            fixed(ROWS, LOCKED, LANES),
            fixed(LANES, LANES),
            fixed(8, LANES),
        ],
        out_specs=[fixed(ROWS, ORBS, LANES), fixed(ORBS, 128)],
        out_shape=[
            jax.ShapeDtypeStruct((ROWS, ORBS, LANES), F32),
            jax.ShapeDtypeStruct((ORBS, 128), F32),
        ],
        scratch_shapes=[
            pltpu.VMEM((ORBS * RH, NB * LANES), F32),
            pltpu.VMEM((NS, 3 * PAIR), BF16),
            pltpu.VMEM((ORBS, ROWS, LANES), F32),
            pltpu.VMEM((16, 24, LANES), F32),
            pltpu.VMEM((8, ORBS * ROWS), F32),
        ],
        compiler_params=pltpu.CompilerParams(vmem_limit_bytes=48 << 20),
        name="apply",
    )(orb, cell, owner, atom, prof, returned, xhalo, yhalo, zhalo, potential, lines, inner, outer)


def total_body(partial, total, stage, slots, send, receive):
    groups = axis_partners()
    meet([shift for group in groups for shift in group])
    value = partial[...]
    everything = []
    base = 0
    for level, group in enumerate(groups):
        stage[level] = value
        sent = reduce_start(stage.at[level], slots, send, receive, base, group)
        everything += sent
        value = reduce_finish(value, slots, base, sent)
        base += len(group)
    total[...] = value
    for copy in everything:
        copy.wait_send()


def whole_sum(partial):
    dma = pltpu.SemaphoreType.DMA
    return pl.pallas_call(
        total_body,
        in_specs=[vmem()],
        out_specs=vmem(),
        out_shape=jax.ShapeDtypeStruct((ORBS, 128), F32),
        scratch_shapes=[
            pltpu.VMEM((3, ORBS, 128), F32),
            pltpu.VMEM((17, ORBS, 128), F32),
            dma((17,)), dma((17,)),
        ],
        compiler_params=pltpu.CompilerParams(collective_id=1, has_side_effects=True),
        name="whole_sum",
    )(partial)


def inverse_of(matrix):
    count = matrix.shape[0]
    columns = lax.broadcasted_iota(jnp.int32, (count, count), 1)
    rows = lax.broadcasted_iota(jnp.int32, (count, count), 0)
    for k in range(count):
        scale = 1.0 / matrix[k : k + 1, k : k + 1]
        column = matrix[:, k : k + 1]
        unit = jnp.where(rows == k, 1.0, 0.0)
        cleared = jnp.where(columns == k, unit, matrix)
        line = cleared[k : k + 1, :] * scale
        matrix = jnp.where(rows == k, line, cleared - column * line)
    return matrix


def inverse_body(gram, inverse):
    packed = gram[...]
    inverse[...] = inverse_of(jnp.concatenate([packed[:, 0:64], packed[:, 64:128]], axis=0))


def inverted(gram):
    return pl.pallas_call(
        inverse_body,
        in_specs=[vmem()],
        out_specs=vmem(),
        out_shape=jax.ShapeDtypeStruct((LOCKED, LOCKED), F32),
        name="inverse",
    )(gram)


GROUP = 4
BLOCK = 32


def project_body(applied, lines, total, inverse, out, mixed):
    @pl.when(pl.program_id(0) == 0)
    def _():
        mixing = jnp.dot(
            total[:, 0:LOCKED], inverse[...], precision=HIGHEST, preferred_element_type=F32
        ).astype(BF16)
        mixed[...] = jnp.zeros_like(mixed)
        for j in range(GROUP):
            mixed[j * ORBS : (j + 1) * ORBS, j * LOCKED : (j + 1) * LOCKED] = mixing.astype(F32)

    weights = mixed[...].astype(BF16)
    for g in range(BLOCK // GROUP):
        four = lines[g * GROUP : (g + 1) * GROUP].reshape(GROUP * LOCKED, LANES)
        fix = jnp.dot(weights, four, preferred_element_type=F32)
        for j in range(GROUP):
            r = g * GROUP + j
            out[:, r, :] = applied[r] - fix[j * ORBS : (j + 1) * ORBS]


def project(applied, lines, total, inverse):
    return pl.pallas_call(
        project_body,
        grid=(ROWS // BLOCK,),
        in_specs=[
            pl.BlockSpec((BLOCK, ORBS, LANES), lambda i: (i, 0, 0)),
            pl.BlockSpec((BLOCK, LOCKED, LANES), lambda i: (i, 0, 0)),
            fixed(ORBS, 128),
            fixed(LOCKED, LOCKED),
        ],
        out_specs=pl.BlockSpec((ORBS, BLOCK, LANES), lambda i: (0, i, 0)),
        out_shape=jax.ShapeDtypeStruct((ORBS, ROWS, LANES), F32),
        scratch_shapes=[pltpu.VMEM((GROUP * ORBS, GROUP * LOCKED), F32)],
        name="project",
    )(applied, lines, total, inverse)


def on_device(
    orbitals, potential, locked, sphere_cell, sphere_owner, sphere_atom,
    sphere_profile, atom_strength, atom_channels,
):
    orb = orbitals.reshape(ORBS, ROWS, LANES)
    cell = sphere_cell.reshape(1, POINTS)
    owner = sphere_owner.reshape(1, POINTS)
    atom = sphere_atom.reshape(1, POINTS)
    prof = sphere_profile.reshape(CHANNELS, POINTS)
    sums, gram, lines, yface, zface, strength = gather(
        orb, cell, owner, atom, prof, locked.reshape(LOCKED, ROWS, LANES),
        atom_strength.reshape(SLOTS, CHANNELS), atom_channels.reshape(1, SLOTS),
    )
    returned, xhalo, yhalo, zhalo, gram = exchange(sums, gram, strength, orb, yface, zface)
    inverse = inverted(gram)
    applied, partial = apply(
        orb, cell, owner, atom, prof, returned, xhalo, yhalo, zhalo,
        potential.reshape(ROWS, LANES), lines,
    )
    total = whole_sum(partial)
    return project(applied, lines, total, inverse).reshape(orbitals.shape)


def solution(mesh):
    placed = (
        P(None, "gx", "gy", "gz"),
        P("gx", "gy", "gz"),
        P(None, "gx", "gy", "gz"),
        P("gx", "gy", "gz", None),
        P("gx", "gy", "gz", None),
        P("gx", "gy", "gz", None),
        P("gx", "gy", "gz", None, None),
        P("gx", "gy", "gz", None, None),
        P("gx", "gy", "gz", None),
    )
    return jax.shard_map(
        on_device, mesh=mesh, in_specs=placed, out_specs=P(None, "gx", "gy", "gz"), check_vma=False
    )
```

```python
import jax
import jax.numpy as jnp
import numpy as np
from jax import lax
from jax.experimental import pallas as pl
from jax.experimental.pallas import tpu as pltpu
from jax.sharding import PartitionSpec as P

STENCIL_WEIGHTS = (-205.0 / 72.0, 8.0 / 5.0, -1.0 / 5.0, 8.0 / 315.0, -1.0 / 560.0)
MESH = pl.DeviceIdType.MESH
F32 = jnp.float32
BF16 = jnp.bfloat16
HIGHEST = lax.Precision.HIGHEST

ORBS = 8
ROWS = 256
LANES = 128
SLOTS = 32
OWNERS = 32
CHANNELS = 9
POINTS = 16384
LOCKED = 64
CHUNK = 1024
STEPS = POINTS // CHUNK
RH = 64
NB = ROWS // RH
PAIR = CHANNELS * OWNERS
NS = ORBS * SLOTS

NT = (((1,), (1,)), ((), ()))
TN = (((0,), (0,)), ((), ()))


def onehot(count, index):
    ids = lax.broadcasted_iota(jnp.int32, (count, index.shape[1]), 0)
    return jnp.where(ids == index, 1.0, 0.0).astype(BF16)


def cell_parts(cell):
    line = cell >> 7
    return cell & (LANES - 1), line & (RH - 1), line // RH


def cell_onehot(lane, block):
    lanes = onehot(LANES, lane)
    blocks = onehot(16, block)
    return jnp.concatenate([lanes * blocks[b : b + 1] for b in range(NB)], axis=0)


def split(value):
    high = value.astype(BF16)
    return high, (value - high.astype(F32)).astype(BF16)


def spread_rows(rows, mask):
    return jnp.concatenate([mask * row for row in rows], axis=0)


def each_row(value):
    return [value[i : i + 1] for i in range(value.shape[0])]


def picked_rows(values, hit, count, height):
    parts = [
        jnp.sum(jnp.where(hit, values[n * height : (n + 1) * height], 0.0), axis=0, keepdims=True)
        for n in range(count)
    ]
    return jnp.concatenate(parts, axis=0)


def offset_of(code):
    return code // 9 - 1, code // 3 % 3 - 1, code % 3 - 1


CODES = [code for code in range(27) if code != 13]


def device(shift):
    spot = []
    for name, move in zip(("gx", "gy", "gz"), shift):
        size = lax.axis_size(name)
        spot.append(lax.rem(lax.axis_index(name) + (move + size), size))
    return tuple(spot)


def axis_partners():
    found = []
    for axis, name in ((2, "gz"), (1, "gy"), (0, "gx")):
        group = []
        for k in range(1, lax.axis_size(name)):
            shift = [0, 0, 0]
            shift[axis] = k
            group.append(tuple(shift))
        found.append(group)
    return found


def canonical(shift):
    sizes = [lax.axis_size(name) for name in ("gx", "gy", "gz")]
    return tuple(move % size for move, size in zip(shift, sizes))


def meet(shifts):
    barrier = pltpu.get_barrier_semaphore()
    for shift in shifts:
        pl.semaphore_signal(barrier, inc=1, device_id=device(shift), device_id_type=MESH)
    pl.semaphore_wait(barrier, len(shifts))


def remote(source, target, send, receive, shift):
    return pltpu.make_async_remote_copy(
        src_ref=source, dst_ref=target, send_sem=send, recv_sem=receive,
        device_id=device(shift), device_id_type=MESH,
    )


def reduce_start(source, slots, send, receive, base, group):
    copies = [
        remote(source, slots.at[base + k], send.at[base + k], receive.at[base + k], shift)
        for k, shift in enumerate(group)
    ]
    for copy in copies:
        copy.start()
    return copies


def reduce_finish(own, slots, base, copies):
    total = own
    for k, copy in enumerate(copies):
        copy.wait_recv()
        total = total + slots[base + k]
    return total


def ids(shape, dimension):
    return lax.broadcasted_iota(jnp.int32, shape, dimension)


def by_distance(distance, centre):
    total = jnp.where(distance == 0, centre, 0.0)
    for k in range(1, 5):
        total = jnp.where(distance == k, -0.5 * STENCIL_WEIGHTS[k], total)
    return total


def exact_dot(left, right, dims=(((1,), (0,)), ((), ()))):
    return lax.dot_general(left, right, dims, precision=HIGHEST, preferred_element_type=F32)


def eliminate(matrix, start, stop):
    columns, rows = ids(matrix.shape, 1), ids(matrix.shape, 0)
    for k in range(start, stop):
        scale = 1.0 / matrix[k : k + 1, k : k + 1]
        column = matrix[:, k : k + 1]
        cleared = jnp.where(columns == k, jnp.where(rows == k, 1.0, 0.0), matrix)
        line = cleared[k : k + 1, :] * scale
        matrix = jnp.where(rows == k, line, cleared - column * line)
    return matrix


def body(
    orb_h, cell_h, owner_h, atom_h, prof_h, locked_h, strength_h, chans_h, potential_h,
    out,
    orb, cell, owner, atom, prof, locked, strength, chans, potential, arrived,
    table, acc, wide, lines, yface, zface, sums, landed, weighted, returned,
    xhalo, yhalo, zhalo, gram, gstage, gslots, back, local, tall, ends, spread, applied,
    cstage, cslots,
    send1, recv1, send2, recv2, sendg, recvg, sendh, recvh, sendc, recvc,
):
    groups = axis_partners()
    everyone = {canonical(offset_of(code)) for code in CODES}
    for group in groups:
        everyone |= {canonical(shift) for shift in group}
    everyone = sorted(everyone)
    barrier = pltpu.get_barrier_semaphore()
    for shift in everyone:
        pl.semaphore_signal(barrier, inc=1, device_id=device(shift), device_id_type=MESH)
    loads = [
        pltpu.make_async_copy(source, target, arrived.at[k])
        for k, (source, target) in enumerate(
            (
                (orb_h, orb), (cell_h, cell), (owner_h, owner), (atom_h, atom), (prof_h, prof),
                (strength_h, strength), (chans_h, chans), (locked_h, locked),
                (potential_h, potential),
            )
        )
    ]
    for load in loads:
        load.start()
    loads[0].wait()

    for n in range(ORBS):
        for b in range(NB):
            table[n * RH : (n + 1) * RH, b * LANES : (b + 1) * LANES] = orb[
                n, b * RH : (b + 1) * RH, :
            ].astype(BF16)
    whole = orb[...].reshape(ORBS * 16, 16, LANES)
    yface[0] = whole[:, 0:4, :]
    yface[1] = whole[:, 12:16, :]
    row, lane_id = ids((8, LANES), 0), ids((8, LANES), 1)
    pick = jnp.where(lane_id == jnp.where(row < 4, row, LANES - 8 + row), 1.0, 0.0)
    edge = exact_dot(pick, orb[...].reshape(ORBS * ROWS, LANES), NT)
    zface[0] = edge[0:4]
    zface[1] = edge[4:8]

    pl.semaphore_wait(barrier, len(everyone))
    halos = [
        remote(orb.at[:, pl.ds(192, 64), :], xhalo.at[0], sendh.at[0], recvh.at[0], (1, 0, 0)),
        remote(orb.at[:, pl.ds(0, 64), :], xhalo.at[1], sendh.at[1], recvh.at[1], (-1, 0, 0)),
        remote(yface.at[1], yhalo.at[0], sendh.at[2], recvh.at[2], (0, 1, 0)),
        remote(yface.at[0], yhalo.at[1], sendh.at[3], recvh.at[3], (0, -1, 0)),
        remote(zface.at[1], zhalo.at[0], sendh.at[4], recvh.at[4], (0, 0, 1)),
        remote(zface.at[0], zhalo.at[1], sendh.at[5], recvh.at[5], (0, 0, -1)),
    ]
    for copy in halos:
        copy.start()
    everything = list(halos)

    for load in loads[1:7]:
        load.wait()
    acc[...] = jnp.zeros_like(acc)

    @pl.loop(0, STEPS)
    def _(step):
        here = pl.ds(pl.multiple_of(step * CHUNK, CHUNK), CHUNK)
        lane, low, block = cell_parts(cell[:, here])
        found = jnp.dot(table[...], cell_onehot(lane, block), preferred_element_type=F32)
        values = picked_rows(found, ids((RH, CHUNK), 0) == low, ORBS, RH).astype(BF16)
        right = spread_rows(each_row(values), onehot(SLOTS, atom[:, here]))
        owners = onehot(OWNERS, owner[:, here])
        parts = [split(prof[p, :, here]) for p in range(CHANNELS)]
        left = jnp.concatenate(
            [spread_rows([part[k] for part in parts], owners) for k in range(2)], axis=0
        )
        acc[0 : 2 * PAIR, 0:NS] += lax.dot_general(left, right, NT, preferred_element_type=F32)

    for p in range(CHANNELS):
        sums[:, p, :] = (
            acc[p * OWNERS : (p + 1) * OWNERS, 0:NS]
            + acc[PAIR + p * OWNERS : PAIR + (p + 1) * OWNERS, 0:NS]
        )
    first = [
        remote(sums.at[c], landed.at[c], send1.at[c], recv1.at[c], offset_of(c)) for c in CODES
    ]
    for copy in first:
        copy.start()
    everything += first

    loads[7].wait()
    gram[...] = jnp.zeros_like(gram)

    @pl.loop(0, 16)
    def _(step):
        here = pl.ds(pl.multiple_of(step * 16, 16), 16)
        wide[...] = locked[:, here, :].astype(F32).reshape(LOCKED * 16, LANES)
        rows = [wide[pl.ds(r, LOCKED, stride=16), :].astype(BF16) for r in range(16)]
        for r in range(16):
            lines[step * 16 + r] = rows[r]
        flat = jnp.concatenate(rows, axis=1)
        gram[...] += lax.dot_general(flat, flat, NT, preferred_element_type=F32)

    gstage[0, :, 0:64] = gram[0:32, :]
    gstage[0, :, 64:128] = gram[32:64, :]
    sent = reduce_start(gstage.at[0], gslots, sendg, recvg, 0, groups[0])
    everything += sent

    channel = ids((CHANNELS, NS), 0).astype(F32)
    copies = jnp.where(ids((SLOTS, NS), 1) % SLOTS == ids((SLOTS, NS), 0), 1.0, 0.0)
    grown = exact_dot(jnp.concatenate([strength[p] for p in range(CHANNELS)], axis=0), copies)
    limit = exact_dot(jnp.broadcast_to(chans[...], (8, SLOTS)).astype(F32), copies)[0:1]
    scale = jnp.where(channel < limit - 0.5, grown, 0.0)

    total = sums[13]
    for code, copy in zip(CODES, first):
        copy.wait_recv()
        total = total + landed[code]
    weighted[...] = total * scale
    second = []
    for code in CODES:
        opposite = tuple(-move for move in offset_of(code))
        copy = remote(weighted, returned.at[code], send2.at[code], recv2.at[code], opposite)
        copy.start()
        second.append(copy)
    returned[13] = weighted[...]
    everything += second

    gtotal = reduce_finish(gstage[0], gslots, 0, sent)
    gstage[1] = gtotal
    sent = reduce_start(gstage.at[1], gslots, sendg, recvg, len(groups[0]), groups[1])
    everything += sent

    loads[8].wait()
    for copy in halos:
        copy.wait_recv()
    ends[0:4] = zhalo[0]
    ends[4:8] = zhalo[1]
    square = (LANES, LANES)
    inner = by_distance(jnp.abs(ids(square, 0) - ids(square, 1)), -1.5 * STENCIL_WEIGHTS[0])
    place = jnp.where(row < 4, row - 4, LANES - 4 + row)
    outer = by_distance(jnp.abs(place - lane_id), 0.0)
    for n in range(ORBS):
        centre = orb[n]
        total = exact_dot(centre, inner)
        total += exact_dot(ends[:, n * ROWS : (n + 1) * ROWS], outer, TN)
        total += potential[...] * centre
        long = jnp.concatenate([xhalo[0, n], centre, xhalo[1, n]], axis=0)
        tall[:, 0:4, :] = yhalo[0, n * 16 : (n + 1) * 16]
        tall[:, 4:20, :] = centre.reshape(16, 16, LANES)
        tall[:, 20:24, :] = yhalo[1, n * 16 : (n + 1) * 16]
        for k in range(1, 5):
            pair = long[64 - 16 * k : 320 - 16 * k] + long[64 + 16 * k : 320 + 16 * k]
            side = tall[:, 4 - k : 20 - k, :] + tall[:, 4 + k : 20 + k, :]
            total += (-0.5 * STENCIL_WEIGHTS[k]) * (pair + side.reshape(ROWS, LANES))
        local[n] = total

    for copy in second:
        copy.wait_recv()
    stacked = [
        jnp.concatenate([returned[0:27, p, :], jnp.zeros((OWNERS - 27, NS), F32)], axis=0)
        for p in range(CHANNELS)
    ]
    high, rest = split(jnp.concatenate(stacked, axis=0).T)
    back[...] = jnp.concatenate([high, rest, high], axis=1)
    spread[...] = jnp.zeros_like(spread)

    def scatter(start, stop):
        @pl.loop(start, stop)
        def _(step):
            here = pl.ds(pl.multiple_of(step * CHUNK, CHUNK), CHUNK)
            lane, low, block = cell_parts(cell[:, here])
            hot = cell_onehot(lane, block)
            owners = onehot(OWNERS, owner[:, here])
            parts = [split(prof[p, :, here]) for p in range(CHANNELS)]
            most = spread_rows([part[0] for part in parts], owners)
            less = spread_rows([part[1] for part in parts], owners)
            near = jnp.dot(
                back[...], jnp.concatenate([most, most, less], axis=0), preferred_element_type=F32
            )
            hit = ids((SLOTS, CHUNK), 0) == atom[:, here]
            terms = picked_rows(near, hit, ORBS, SLOTS).astype(BF16)
            spread[...] += lax.dot_general(
                spread_rows(each_row(terms), onehot(RH, low)), hot, NT, preferred_element_type=F32
            )

    scatter(0, STEPS // 2)
    base = len(groups[0])
    gtotal = reduce_finish(gtotal, gslots, base, sent)
    gstage[2] = gtotal
    base += len(groups[1])
    sent = reduce_start(gstage.at[2], gslots, sendg, recvg, base, groups[2])
    everything += sent
    scatter(STEPS // 2, STEPS)

    for n in range(ORBS):
        for b in range(NB):
            applied[b * RH : (b + 1) * RH, n, :] = (
                local[n, b * RH : (b + 1) * RH, :]
                + spread[n * RH : (n + 1) * RH, b * LANES : (b + 1) * LANES]
            )
    value = jnp.zeros((ORBS, LOCKED), F32)
    for g in range(ROWS // 16):
        mine = jnp.concatenate([applied[g * 16 + r].astype(BF16) for r in range(16)], axis=1)
        kept = jnp.concatenate([lines[g * 16 + r] for r in range(16)], axis=1)
        value += lax.dot_general(mine, kept, NT, preferred_element_type=F32)
    value = jnp.concatenate([value, jnp.zeros((ORBS, 128 - LOCKED), F32)], axis=1)

    cstage[0] = value
    csent = reduce_start(cstage.at[0], cslots, sendc, recvc, 0, groups[0])
    everything += csent
    packed = reduce_finish(gtotal, gslots, base, sent)
    matrix = jnp.concatenate([packed[:, 0:64], packed[:, 64:128]], axis=0)
    matrix = eliminate(matrix, 0, 22)
    base = 0
    for level, stop in enumerate((43, LOCKED, LOCKED)):
        value = reduce_finish(value, cslots, base, csent)
        base += len(groups[level])
        if level < 2:
            cstage[level + 1] = value
            csent = reduce_start(
                cstage.at[level + 1], cslots, sendc, recvc, base, groups[level + 1]
            )
            everything += csent
            matrix = eliminate(matrix, (22, 43)[level], stop)

    mixing = exact_dot(value[:, 0:LOCKED], matrix).astype(BF16).astype(F32)
    aside = jnp.zeros((ORBS, LOCKED), F32)
    weights = jnp.concatenate(
        [
            jnp.concatenate([mixing if i == j else aside for i in range(4)], axis=1)
            for j in range(4)
        ],
        axis=0,
    ).astype(BF16)
    @pl.loop(0, 8)
    def _(step):
        for g in range(4):
            first_row = step * 32 + g * 8
            sides = [
                lines[pl.ds(first_row + 4 * h, 4)].reshape(4 * LOCKED, LANES) for h in range(2)
            ]
            fix = jnp.dot(weights, jnp.concatenate(sides, axis=1), preferred_element_type=F32)
            for h in range(2):
                for j in range(4):
                    r = first_row + 4 * h + j
                    out[:, r, :] = (
                        applied[r] - fix[j * ORBS : (j + 1) * ORBS, h * LANES : (h + 1) * LANES]
                    )

    for copy in everything:
        copy.wait_send()


def on_device(
    orbitals, potential, locked, sphere_cell, sphere_owner, sphere_atom,
    sphere_profile, atom_strength, atom_channels,
):
    dma = pltpu.SemaphoreType.DMA
    shapes = (
        ((ORBS, ROWS, LANES), F32), ((1, POINTS), jnp.int32), ((1, POINTS), jnp.int32),
        ((1, POINTS), jnp.int32), ((CHANNELS, 1, POINTS), F32), ((LOCKED, ROWS, LANES), BF16),
        ((CHANNELS, 1, SLOTS), F32), ((1, SLOTS), jnp.int32), ((ROWS, LANES), F32),
    )
    work = (
        ((ORBS * RH, NB * LANES), BF16), ((2 * PAIR, NS), F32), ((LOCKED * 16, LANES), F32),
        ((ROWS, LOCKED, LANES), BF16), ((2, ORBS * 16, 4, LANES), F32),
        ((2, 4, ORBS * ROWS), F32), ((OWNERS, CHANNELS, NS), F32), ((27, CHANNELS, NS), F32),
        ((CHANNELS, NS), F32), ((27, CHANNELS, NS), F32), ((2, ORBS, 64, LANES), F32),
        ((2, ORBS * 16, 4, LANES), F32), ((2, 4, ORBS * ROWS), F32), ((LOCKED, LOCKED), F32),
        ((3, 32, 128), F32), ((17, 32, 128), F32), ((NS, 3 * PAIR), BF16),
        ((ORBS, ROWS, LANES), F32), ((16, 24, LANES), F32), ((8, ORBS * ROWS), F32),
        ((ORBS * RH, NB * LANES), F32), ((ROWS, ORBS, LANES), F32), ((3, ORBS, 128), F32),
        ((17, ORBS, 128), F32),
    )
    out = pl.pallas_call(
        body,
        in_specs=[pl.BlockSpec(memory_space=pl.ANY)] * 9,
        out_specs=pl.BlockSpec(memory_space=pltpu.VMEM),
        out_shape=jax.ShapeDtypeStruct((ORBS, ROWS, LANES), F32),
        scratch_shapes=[pltpu.VMEM(*shape) for shape in shapes]
        + [dma((9,))]
        + [pltpu.VMEM(*shape) for shape in work]
        + [dma((count,)) for count in (27, 27, 27, 27, 17, 17, 6, 6, 17, 17)],
        compiler_params=pltpu.CompilerParams(
            collective_id=0, has_side_effects=True, vmem_limit_bytes=56 << 20
        ),
        name="apply_and_project",
    )(
        orbitals.reshape(ORBS, ROWS, LANES),
        sphere_cell.reshape(1, POINTS),
        sphere_owner.reshape(1, POINTS),
        sphere_atom.reshape(1, POINTS),
        sphere_profile.reshape(CHANNELS, 1, POINTS),
        locked.reshape(LOCKED, ROWS, LANES),
        jnp.transpose(atom_strength, (0, 1, 4, 2, 3)).reshape(CHANNELS, 1, SLOTS),
        atom_channels.reshape(1, SLOTS),
        potential.reshape(ROWS, LANES),
    )
    return out.reshape(orbitals.shape)


def solution(mesh):
    placed = (
        P(None, "gx", "gy", "gz"),
        P("gx", "gy", "gz"),
        P(None, "gx", "gy", "gz"),
        P("gx", "gy", "gz", None),
        P("gx", "gy", "gz", None),
        P("gx", "gy", "gz", None),
        P("gx", "gy", "gz", None, None),
        P("gx", "gy", "gz", None, None),
        P("gx", "gy", "gz", None),
    )
    return jax.shard_map(
        on_device, mesh=mesh, in_specs=placed, out_specs=P(None, "gx", "gy", "gz"), check_vma=False
    )
```

```python
import jax
import jax.numpy as jnp
import numpy as np
from jax import lax
from jax.experimental import pallas as pl
from jax.experimental.pallas import tpu as pltpu
from jax.sharding import PartitionSpec as P

STENCIL_WEIGHTS = (-205.0 / 72.0, 8.0 / 5.0, -1.0 / 5.0, 8.0 / 315.0, -1.0 / 560.0)
MESH = pl.DeviceIdType.MESH
F32 = jnp.float32
BF16 = jnp.bfloat16
HIGHEST = lax.Precision.HIGHEST

ORBS = 8
ROWS = 256
LANES = 128
SLOTS = 32
OWNERS = 32
CHANNELS = 9
POINTS = 16384
LOCKED = 64
CHUNK = 1024
STEPS = POINTS // CHUNK
RH = 64
NB = ROWS // RH
PAIR = CHANNELS * OWNERS
NS = ORBS * SLOTS

NT = (((1,), (1,)), ((), ()))
TN = (((0,), (0,)), ((), ()))


def onehot(count, index):
    ids = lax.broadcasted_iota(jnp.int32, (count, index.shape[1]), 0)
    return jnp.where(ids == index, 1.0, 0.0).astype(BF16)


def cell_parts(cell):
    line = cell >> 7
    return cell & (LANES - 1), line & (RH - 1), line // RH


def cell_onehot(lane, block):
    lanes = onehot(LANES, lane)
    blocks = onehot(16, block)
    return jnp.concatenate([lanes * blocks[b : b + 1] for b in range(NB)], axis=0)


def split(value):
    high = value.astype(BF16)
    return high, (value - high.astype(F32)).astype(BF16)


def spread_rows(rows, mask):
    return jnp.concatenate([mask * row for row in rows], axis=0)


def each_row(value):
    return [value[i : i + 1] for i in range(value.shape[0])]


def picked_rows(values, hit, count, height):
    parts = [
        jnp.sum(jnp.where(hit, values[n * height : (n + 1) * height], 0.0), axis=0, keepdims=True)
        for n in range(count)
    ]
    return jnp.concatenate(parts, axis=0)


def offset_of(code):
    return code // 9 - 1, code // 3 % 3 - 1, code % 3 - 1


CODES = sorted(
    (code for code in range(27) if code != 13),
    key=lambda code: -sum(abs(move) for move in offset_of(code)),
)


def device(shift):
    spot = []
    for name, move in zip(("gx", "gy", "gz"), shift):
        size, mine = lax.axis_size(name), lax.axis_index(name)
        if move == "flip":
            spot.append(mine + 1 - 2 * lax.rem(mine, 2))
        else:
            spot.append(lax.rem(mine + move % size, size))
    return tuple(spot)


def quick_partners():
    one, two = [], []
    for k in range(lax.axis_size("gz")):
        one += [(0, 0, k), ("flip", 0, k)]
    for k in range(lax.axis_size("gy")):
        two += [(0, k, 0), (lax.axis_size("gx") // 2, k, 0)]
    return one[1:], two[1:]


def axis_partners():
    found = []
    for axis, name in ((2, "gz"), (1, "gy"), (0, "gx")):
        group = []
        for k in range(1, lax.axis_size(name)):
            shift = [0, 0, 0]
            shift[axis] = k
            group.append(tuple(shift))
        found.append(group)
    return found


def canonical(shift):
    sizes = [lax.axis_size(name) for name in ("gx", "gy", "gz")]
    return tuple(move if move == "flip" else move % size for move, size in zip(shift, sizes))


def remote(source, target, send, receive, shift):
    return pltpu.make_async_remote_copy(
        src_ref=source, dst_ref=target, send_sem=send, recv_sem=receive,
        device_id=device(shift), device_id_type=MESH,
    )


def reduce_start(source, slots, send, receive, base, group):
    copies = [
        remote(source, slots.at[base + k], send.at[base + k], receive.at[base + k], shift)
        for k, shift in enumerate(group)
    ]
    for copy in copies:
        copy.start()
    return copies


def reduce_finish(own, slots, base, copies):
    total = own
    for k, copy in enumerate(copies):
        copy.wait_recv()
        total = total + slots[base + k]
    return total


def ids(shape, dimension):
    return lax.broadcasted_iota(jnp.int32, shape, dimension)


def by_distance(distance, centre):
    total = jnp.where(distance == 0, centre, 0.0)
    for k in range(1, 5):
        total = jnp.where(distance == k, -0.5 * STENCIL_WEIGHTS[k], total)
    return total


def exact_dot(left, right, dims=(((1,), (0,)), ((), ()))):
    return lax.dot_general(left, right, dims, precision=HIGHEST, preferred_element_type=F32)


def eliminate(matrix, start, stop):
    columns, rows = ids(matrix.shape, 1), ids(matrix.shape, 0)
    for k in range(start, stop):
        scale = 1.0 / matrix[k : k + 1, k : k + 1]
        column = matrix[:, k : k + 1]
        cleared = jnp.where(columns == k, jnp.where(rows == k, 1.0, 0.0), matrix)
        line = cleared[k : k + 1, :] * scale
        matrix = jnp.where(rows == k, line, cleared - column * line)
    return matrix


def body(
    orb_h, cell_h, owner_h, atom_h, prof_h, locked_h, strength_h, chans_h, potential_h,
    out,
    orb, cell, owner, atom, prof, locked, strength, chans, potential, arrived,
    table, acc, wide, lines, yface, zface, sums, landed, weighted, returned,
    xhalo, yhalo, zhalo, gram, gstage, gslots, back, local, tall, ends, spread, applied,
    cstage, cslots,
    send1, recv1, send2, recv2, sendg, recvg, sendh, recvh, sendc, recvc,
):
    groups = axis_partners()
    everyone = {canonical(offset_of(code)) for code in CODES}
    quick = quick_partners()
    for group in groups + list(quick):
        everyone |= {canonical(shift) for shift in group}
    near = {0, 1, lax.axis_size("gz") - 1}
    everyone = [shift for shift in everyone if shift[0] != "flip" or shift[2] not in near]
    everyone = sorted(everyone, key=str)
    loads = [
        pltpu.make_async_copy(source, target, arrived.at[k])
        for k, (source, target) in enumerate(
            (
                (orb_h, orb), (cell_h, cell), (owner_h, owner), (atom_h, atom), (prof_h, prof),
                (strength_h, strength), (chans_h, chans), (locked_h, locked),
                (potential_h, potential),
            )
        )
    ]
    for load in loads:
        load.start()
    barrier = pltpu.get_barrier_semaphore()
    for shift in everyone:
        pl.semaphore_signal(barrier, inc=1, device_id=device(shift), device_id_type=MESH)
    loads[0].wait()

    for n in range(ORBS):
        for b in range(NB):
            table[n * RH : (n + 1) * RH, b * LANES : (b + 1) * LANES] = orb[
                n, b * RH : (b + 1) * RH, :
            ].astype(BF16)
    for load in loads[1:7]:
        load.wait()
    acc[...] = jnp.zeros_like(acc)

    def collect(start, stop, side=None):
        @pl.loop(start, stop)
        def _(step):
            here = pl.ds(pl.multiple_of(step * CHUNK, CHUNK), CHUNK)
            lane, low, block = cell_parts(cell[:, here])
            found = jnp.dot(table[...], cell_onehot(lane, block), preferred_element_type=F32)
            values = picked_rows(found, ids((RH, CHUNK), 0) == low, ORBS, RH).astype(BF16)
            right = spread_rows(each_row(values), onehot(SLOTS, atom[:, here]))
            owners = onehot(OWNERS, owner[:, here])
            parts = [split(prof[p, :, here]) for p in range(CHANNELS)]
            left = jnp.concatenate(
                [spread_rows([part[k] for part in parts], owners) for k in range(2)], axis=0
            )
            acc[0 : 2 * PAIR, 0:NS] += lax.dot_general(left, right, NT, preferred_element_type=F32)
            if side is not None:
                side(step - start)

    def locked_rows(step):
        here = pl.ds(pl.multiple_of(step * 32, 32), 32)
        wide[...] = locked[:, here, :].astype(F32).reshape(LOCKED * 32, LANES)
        rows = [wide[pl.ds(r, LOCKED, stride=32), :].astype(BF16) for r in range(32)]
        for r in range(32):
            lines[step * 32 + r] = rows[r]
        flat = jnp.concatenate(rows, axis=1)
        gram[...] += lax.dot_general(flat, flat, NT, preferred_element_type=F32)

    collect(0, 2)
    whole = orb[...].reshape(ORBS * 16, 16, LANES)
    yface[0] = whole[:, 0:4, :]
    yface[1] = whole[:, 12:16, :]
    row, lane_id = ids((8, LANES), 0), ids((8, LANES), 1)
    pick = jnp.where(lane_id == jnp.where(row < 4, row, LANES - 8 + row), 1.0, 0.0)
    edge = exact_dot(pick, orb[...].reshape(ORBS * ROWS, LANES), NT)
    zface[0] = edge[0:4]
    zface[1] = edge[4:8]

    pl.semaphore_wait(barrier, len(everyone))
    halos = [
        remote(orb.at[:, pl.ds(192, 64), :], xhalo.at[0], sendh.at[0], recvh.at[0], (1, 0, 0)),
        remote(orb.at[:, pl.ds(0, 64), :], xhalo.at[1], sendh.at[1], recvh.at[1], (-1, 0, 0)),
        remote(yface.at[1], yhalo.at[0], sendh.at[2], recvh.at[2], (0, 1, 0)),
        remote(yface.at[0], yhalo.at[1], sendh.at[3], recvh.at[3], (0, -1, 0)),
        remote(zface.at[1], zhalo.at[0], sendh.at[4], recvh.at[4], (0, 0, 1)),
        remote(zface.at[0], zhalo.at[1], sendh.at[5], recvh.at[5], (0, 0, -1)),
    ]
    for copy in halos:
        copy.start()
    everything = list(halos)

    loads[7].wait()
    gram[...] = jnp.zeros_like(gram)
    collect(2, 10, locked_rows)
    gstage[0, :, 0:64] = gram[0:32, :]
    gstage[0, :, 64:128] = gram[32:64, :]
    sent = reduce_start(gstage.at[0], gslots, sendg, recvg, 0, groups[0])
    everything += sent
    collect(10, 13)
    gtotal = reduce_finish(gstage[0], gslots, 0, sent)
    gstage[1] = gtotal
    base = len(groups[0])
    sent = reduce_start(gstage.at[1], gslots, sendg, recvg, base, groups[1])
    everything += sent
    collect(13, STEPS)
    gtotal = reduce_finish(gtotal, gslots, base, sent)
    gstage[2] = gtotal
    base += len(groups[1])
    sent = reduce_start(gstage.at[2], gslots, sendg, recvg, base, groups[2])
    everything += sent

    for p in range(CHANNELS):
        sums[:, p, :] = (
            acc[p * OWNERS : (p + 1) * OWNERS, 0:NS]
            + acc[PAIR + p * OWNERS : PAIR + (p + 1) * OWNERS, 0:NS]
        )
    first = [
        remote(sums.at[c], landed.at[c], send1.at[c], recv1.at[c], offset_of(c)) for c in CODES
    ]
    for copy in first:
        copy.start()
    everything += first

    packed = reduce_finish(gtotal, gslots, base, sent)
    matrix = jnp.concatenate([packed[:, 0:64], packed[:, 64:128]], axis=0)
    gram[...] = eliminate(matrix, 0, LOCKED)

    channel = ids((CHANNELS, NS), 0).astype(F32)
    copies = jnp.where(ids((SLOTS, NS), 1) % SLOTS == ids((SLOTS, NS), 0), 1.0, 0.0)
    grown = exact_dot(jnp.concatenate([strength[p] for p in range(CHANNELS)], axis=0), copies)
    limit = exact_dot(jnp.broadcast_to(chans[...], (8, SLOTS)).astype(F32), copies)[0:1]
    scale = jnp.where(channel < limit - 0.5, grown, 0.0)

    total = sums[13]
    for code, copy in zip(CODES, first):
        copy.wait_recv()
        total = total + landed[code]
    weighted[...] = total * scale
    second = []
    for code in CODES:
        opposite = tuple(-move for move in offset_of(code))
        copy = remote(weighted, returned.at[code], send2.at[code], recv2.at[code], opposite)
        copy.start()
        second.append(copy)
    returned[13] = weighted[...]
    everything += second

    loads[8].wait()
    for copy in halos:
        copy.wait_recv()
    ends[0:4] = zhalo[0]
    ends[4:8] = zhalo[1]
    square = (LANES, LANES)
    inner = by_distance(jnp.abs(ids(square, 0) - ids(square, 1)), -1.5 * STENCIL_WEIGHTS[0])
    place = jnp.where(row < 4, row - 4, LANES - 4 + row)
    outer = by_distance(jnp.abs(place - lane_id), 0.0)
    for n in range(ORBS):
        centre = orb[n]
        total = exact_dot(centre, inner)
        total += exact_dot(ends[:, n * ROWS : (n + 1) * ROWS], outer, TN)
        total += potential[...] * centre
        long = jnp.concatenate([xhalo[0, n], centre, xhalo[1, n]], axis=0)
        tall[:, 0:4, :] = yhalo[0, n * 16 : (n + 1) * 16]
        tall[:, 4:20, :] = centre.reshape(16, 16, LANES)
        tall[:, 20:24, :] = yhalo[1, n * 16 : (n + 1) * 16]
        for k in range(1, 5):
            pair = long[64 - 16 * k : 320 - 16 * k] + long[64 + 16 * k : 320 + 16 * k]
            side = tall[:, 4 - k : 20 - k, :] + tall[:, 4 + k : 20 + k, :]
            total += (-0.5 * STENCIL_WEIGHTS[k]) * (pair + side.reshape(ROWS, LANES))
        local[n] = total

    for copy in second:
        copy.wait_recv()
    stacked = [
        jnp.concatenate([returned[0:27, p, :], jnp.zeros((OWNERS - 27, NS), F32)], axis=0)
        for p in range(CHANNELS)
    ]
    high, rest = split(jnp.concatenate(stacked, axis=0).T)
    back[...] = jnp.concatenate([high, rest, high], axis=1)
    spread[...] = jnp.zeros_like(spread)

    def scatter(start, stop):
        @pl.loop(start, stop)
        def _(step):
            here = pl.ds(pl.multiple_of(step * CHUNK, CHUNK), CHUNK)
            lane, low, block = cell_parts(cell[:, here])
            hot = cell_onehot(lane, block)
            owners = onehot(OWNERS, owner[:, here])
            parts = [split(prof[p, :, here]) for p in range(CHANNELS)]
            most = spread_rows([part[0] for part in parts], owners)
            less = spread_rows([part[1] for part in parts], owners)
            near = jnp.dot(
                back[...], jnp.concatenate([most, most, less], axis=0), preferred_element_type=F32
            )
            hit = ids((SLOTS, CHUNK), 0) == atom[:, here]
            terms = picked_rows(near, hit, ORBS, SLOTS).astype(BF16)
            spread[...] += lax.dot_general(
                spread_rows(each_row(terms), onehot(RH, low)), hot, NT, preferred_element_type=F32
            )

    scatter(0, STEPS)

    for n in range(ORBS):
        for b in range(NB):
            applied[b * RH : (b + 1) * RH, n, :] = (
                local[n, b * RH : (b + 1) * RH, :]
                + spread[n * RH : (n + 1) * RH, b * LANES : (b + 1) * LANES]
            )
    value = jnp.zeros((ORBS, LOCKED), F32)
    for g in range(ROWS // 16):
        mine = jnp.concatenate([applied[g * 16 + r].astype(BF16) for r in range(16)], axis=1)
        kept = jnp.concatenate([lines[g * 16 + r] for r in range(16)], axis=1)
        value += lax.dot_general(mine, kept, NT, preferred_element_type=F32)
    value = jnp.concatenate([value, jnp.zeros((ORBS, 128 - LOCKED), F32)], axis=1)

    base = 0
    for level, group in enumerate(quick):
        cstage[level] = value
        csent = reduce_start(cstage.at[level], cslots, sendc, recvc, base, group)
        everything += csent
        value = reduce_finish(value, cslots, base, csent)
        base += len(group)

    mixing = exact_dot(value[:, 0:LOCKED], gram[...]).astype(BF16).astype(F32)
    aside = jnp.zeros((ORBS, LOCKED), F32)
    weights = jnp.concatenate(
        [
            jnp.concatenate([mixing if i == j else aside for i in range(4)], axis=1)
            for j in range(4)
        ],
        axis=0,
    ).astype(BF16)
    @pl.loop(0, 2)
    def _(step):
        for g in range(16):
            first_row = step * 128 + g * 8
            sides = [
                lines[pl.ds(first_row + 4 * h, 4)].reshape(4 * LOCKED, LANES) for h in range(2)
            ]
            fix = jnp.dot(weights, jnp.concatenate(sides, axis=1), preferred_element_type=F32)
            for h in range(2):
                for j in range(4):
                    r = first_row + 4 * h + j
                    out[:, r, :] = (
                        applied[r] - fix[j * ORBS : (j + 1) * ORBS, h * LANES : (h + 1) * LANES]
                    )

    for copy in everything:
        copy.wait_send()


def on_device(
    orbitals, potential, locked, sphere_cell, sphere_owner, sphere_atom,
    sphere_profile, atom_strength, atom_channels,
):
    dma = pltpu.SemaphoreType.DMA
    shapes = (
        ((ORBS, ROWS, LANES), F32), ((1, POINTS), jnp.int32), ((1, POINTS), jnp.int32),
        ((1, POINTS), jnp.int32), ((CHANNELS, 1, POINTS), F32), ((LOCKED, ROWS, LANES), BF16),
        ((CHANNELS, 1, SLOTS), F32), ((1, SLOTS), jnp.int32), ((ROWS, LANES), F32),
    )
    work = (
        ((ORBS * RH, NB * LANES), BF16), ((2 * PAIR, NS), F32), ((LOCKED * 32, LANES), F32),
        ((ROWS, LOCKED, LANES), BF16), ((2, ORBS * 16, 4, LANES), F32),
        ((2, 4, ORBS * ROWS), F32), ((OWNERS, CHANNELS, NS), F32), ((27, CHANNELS, NS), F32),
        ((CHANNELS, NS), F32), ((27, CHANNELS, NS), F32), ((2, ORBS, 64, LANES), F32),
        ((2, ORBS * 16, 4, LANES), F32), ((2, 4, ORBS * ROWS), F32), ((LOCKED, LOCKED), F32),
        ((3, 32, 128), F32), ((17, 32, 128), F32), ((NS, 3 * PAIR), BF16),
        ((ORBS, ROWS, LANES), F32), ((16, 24, LANES), F32), ((8, ORBS * ROWS), F32),
        ((ORBS * RH, NB * LANES), F32), ((ROWS, ORBS, LANES), F32), ((2, ORBS, 128), F32),
        ((30, ORBS, 128), F32),
    )
    out = pl.pallas_call(
        body,
        in_specs=[pl.BlockSpec(memory_space=pltpu.HBM)] * 9,
        out_specs=pl.BlockSpec(memory_space=pltpu.VMEM),
        out_shape=jax.ShapeDtypeStruct((ORBS, ROWS, LANES), F32),
        scratch_shapes=[pltpu.VMEM(*shape) for shape in shapes]
        + [dma((9,))]
        + [pltpu.VMEM(*shape) for shape in work]
        + [dma((count,)) for count in (27, 27, 27, 27, 17, 17, 6, 6, 30, 30)],
        compiler_params=pltpu.CompilerParams(
            collective_id=0, has_side_effects=True, vmem_limit_bytes=36 << 20
        ),
        name="apply_and_project",
    )(*(pltpu.with_memory_space_constraint(array, pltpu.HBM) for array in (
        orbitals.reshape(ORBS, ROWS, LANES),
        sphere_cell.reshape(1, POINTS),
        sphere_owner.reshape(1, POINTS),
        sphere_atom.reshape(1, POINTS),
        sphere_profile.reshape(CHANNELS, 1, POINTS),
        locked.reshape(LOCKED, ROWS, LANES),
        jnp.transpose(atom_strength, (0, 1, 4, 2, 3)).reshape(CHANNELS, 1, SLOTS),
        atom_channels.reshape(1, SLOTS),
        potential.reshape(ROWS, LANES),
    )))
    return out.reshape(orbitals.shape)


def solution(mesh):
    placed = (
        P(None, "gx", "gy", "gz"),
        P("gx", "gy", "gz"),
        P(None, "gx", "gy", "gz"),
        P("gx", "gy", "gz", None),
        P("gx", "gy", "gz", None),
        P("gx", "gy", "gz", None),
        P("gx", "gy", "gz", None, None),
        P("gx", "gy", "gz", None, None),
        P("gx", "gy", "gz", None),
    )
    return jax.shard_map(
        on_device, mesh=mesh, in_specs=placed, out_specs=P(None, "gx", "gy", "gz"), check_vma=False
    )
```

```python
import jax
import jax.numpy as jnp
import numpy as np
from jax import lax
from jax.experimental import pallas as pl
from jax.experimental.pallas import tpu as pltpu
from jax.sharding import PartitionSpec as P

STENCIL_WEIGHTS = (-205.0 / 72.0, 8.0 / 5.0, -1.0 / 5.0, 8.0 / 315.0, -1.0 / 560.0)
MESH = pl.DeviceIdType.MESH
F32 = jnp.float32
BF16 = jnp.bfloat16
HIGHEST = lax.Precision.HIGHEST

ORBS = 8
ROWS = 256
LANES = 128
SLOTS = 32
OWNERS = 32
CHANNELS = 9
POINTS = 16384
LOCKED = 64
CHUNK = 4096
STEPS = POINTS // CHUNK
RH = 64
NB = ROWS // RH
PAIR = CHANNELS * OWNERS
NS = ORBS * SLOTS

NT = (((1,), (1,)), ((), ()))
TN = (((0,), (0,)), ((), ()))


def onehot(count, index):
    ids = lax.broadcasted_iota(jnp.int32, (count, index.shape[1]), 0)
    return jnp.where(ids == index, 1.0, 0.0).astype(BF16)


def cell_parts(cell):
    line = cell >> 7
    return cell & (LANES - 1), line & (RH - 1), line // RH


def cell_onehot(lane, block):
    lanes = onehot(LANES, lane)
    blocks = onehot(16, block)
    return jnp.concatenate([lanes * blocks[b : b + 1] for b in range(NB)], axis=0)


def split(value):
    high = value.astype(BF16)
    return high, (value - high.astype(F32)).astype(BF16)


def spread_rows(rows, mask):
    return jnp.concatenate([mask * row for row in rows], axis=0)


def each_row(value):
    return [value[i : i + 1] for i in range(value.shape[0])]


def picked_rows(values, hit, count, height):
    parts = [
        jnp.sum(jnp.where(hit, values[n * height : (n + 1) * height], 0.0), axis=0, keepdims=True)
        for n in range(count)
    ]
    return jnp.concatenate(parts, axis=0)


def offset_of(code):
    return code // 9 - 1, code // 3 % 3 - 1, code % 3 - 1


CODES = sorted(
    (code for code in range(27) if code != 13),
    key=lambda code: -sum(abs(move) for move in offset_of(code)),
)


def device(shift):
    spot = []
    for name, move in zip(("gx", "gy", "gz"), shift):
        size, mine = lax.axis_size(name), lax.axis_index(name)
        if move == "flip":
            spot.append(mine + 1 - 2 * lax.rem(mine, 2))
        else:
            spot.append(lax.rem(mine + move % size, size))
    return tuple(spot)


def quick_partners():
    one, two = [], []
    for k in range(lax.axis_size("gz")):
        one += [(0, 0, k), ("flip", 0, k)]
    for k in range(lax.axis_size("gy")):
        two += [(0, k, 0), (lax.axis_size("gx") // 2, k, 0)]
    return one[1:], two[1:]


def axis_partners():
    found = []
    for axis, name in ((2, "gz"), (1, "gy"), (0, "gx")):
        group = []
        for k in range(1, lax.axis_size(name)):
            shift = [0, 0, 0]
            shift[axis] = k
            group.append(tuple(shift))
        found.append(group)
    return found


def canonical(shift):
    sizes = [lax.axis_size(name) for name in ("gx", "gy", "gz")]
    return tuple(move if move == "flip" else move % size for move, size in zip(shift, sizes))


def remote(source, target, send, receive, shift):
    return pltpu.make_async_remote_copy(
        src_ref=source, dst_ref=target, send_sem=send, recv_sem=receive,
        device_id=device(shift), device_id_type=MESH,
    )


def reduce_start(source, slots, send, receive, base, group):
    copies = [
        remote(source, slots.at[base + k], send.at[base + k], receive.at[base + k], shift)
        for k, shift in enumerate(group)
    ]
    for copy in copies:
        copy.start()
    return copies


def reduce_finish(own, slots, base, copies):
    total = own
    for k, copy in enumerate(copies):
        copy.wait_recv()
        total = total + slots[base + k]
    return total


def ids(shape, dimension):
    return lax.broadcasted_iota(jnp.int32, shape, dimension)


def by_distance(distance, centre):
    total = jnp.where(distance == 0, centre, 0.0)
    for k in range(1, 5):
        total = jnp.where(distance == k, -0.5 * STENCIL_WEIGHTS[k], total)
    return total


def exact_dot(left, right, dims=(((1,), (0,)), ((), ()))):
    return lax.dot_general(left, right, dims, precision=HIGHEST, preferred_element_type=F32)


def eliminate(matrix, start, stop):
    columns, rows = ids(matrix.shape, 1), ids(matrix.shape, 0)
    for k in range(start, stop):
        scale = 1.0 / matrix[k : k + 1, k : k + 1]
        column = matrix[:, k : k + 1]
        cleared = jnp.where(columns == k, jnp.where(rows == k, 1.0, 0.0), matrix)
        line = cleared[k : k + 1, :] * scale
        matrix = jnp.where(rows == k, line, cleared - column * line)
    return matrix


def body(
    orb_h, cell_h, owner_h, atom_h, prof_h, locked_h, strength_h, chans_h, potential_h,
    out,
    orb, cell, owner, atom, prof, locked, strength, chans, potential, arrived,
    table, acc, wide, lines, yface, zface, sums, landed, weighted, returned,
    xhalo, yhalo, zhalo, gram, gstage, gslots, back, local, tall, ends, spread, applied,
    cstage, cslots,
    send1, recv1, send2, recv2, sendg, recvg, sendh, recvh, sendc, recvc,
):
    groups = axis_partners()
    everyone = {canonical(offset_of(code)) for code in CODES}
    quick = quick_partners()
    for group in groups + list(quick):
        everyone |= {canonical(shift) for shift in group}
    near = {0, 1, lax.axis_size("gz") - 1}
    everyone = [shift for shift in everyone if shift[0] != "flip" or shift[2] not in near]
    everyone = sorted(everyone, key=str)
    loads = [
        pltpu.make_async_copy(source, target, arrived.at[k])
        for k, (source, target) in enumerate(
            (
                (orb_h, orb), (cell_h, cell), (owner_h, owner), (atom_h, atom), (prof_h, prof),
                (strength_h, strength), (chans_h, chans), (locked_h, locked),
                (potential_h, potential),
            )
        )
    ]
    for load in loads:
        load.start()
    barrier = pltpu.get_barrier_semaphore()
    for shift in everyone:
        pl.semaphore_signal(barrier, inc=1, device_id=device(shift), device_id_type=MESH)
    loads[0].wait()

    for n in range(ORBS):
        for b in range(NB):
            table[n * RH : (n + 1) * RH, b * LANES : (b + 1) * LANES] = orb[
                n, b * RH : (b + 1) * RH, :
            ].astype(BF16)
    for load in loads[1:7]:
        load.wait()
    acc[...] = jnp.zeros_like(acc)

    def collect(start, stop, side=None):
        @pl.loop(start, stop)
        def _(step):
            here = pl.ds(pl.multiple_of(step * CHUNK, CHUNK), CHUNK)
            lane, low, block = cell_parts(cell[:, here])
            found = jnp.dot(table[...], cell_onehot(lane, block), preferred_element_type=F32)
            values = picked_rows(found, ids((RH, CHUNK), 0) == low, ORBS, RH).astype(BF16)
            right = spread_rows(each_row(values), onehot(SLOTS, atom[:, here]))
            owners = onehot(OWNERS, owner[:, here])
            parts = [split(prof[p, :, here]) for p in range(CHANNELS)]
            left = jnp.concatenate(
                [spread_rows([part[k] for part in parts], owners) for k in range(2)], axis=0
            )
            acc[0 : 2 * PAIR, 0:NS] += lax.dot_general(left, right, NT, preferred_element_type=F32)
            if side is not None:
                side(step - start)

    def locked_rows(step):
        for part in range(8):
            here = pl.ds(pl.multiple_of(step * 128 + part * 16, 16), 16)
            room = wide.at[pl.ds((part % 2) * 1024, 1024)]
            room[...] = locked[:, here, :].astype(F32).reshape(LOCKED * 16, LANES)
            rows = [room[pl.ds(r, LOCKED, stride=16), :].astype(BF16) for r in range(16)]
            for r in range(16):
                lines[step * 128 + part * 16 + r] = rows[r]
            flat = jnp.concatenate(rows, axis=1)
            gram[...] += lax.dot_general(flat, flat, NT, preferred_element_type=F32)

    collect(0, 1)
    whole = orb[...].reshape(ORBS * 16, 16, LANES)
    yface[0] = whole[:, 0:4, :]
    yface[1] = whole[:, 12:16, :]
    row, lane_id = ids((8, LANES), 0), ids((8, LANES), 1)
    pick = jnp.where(lane_id == jnp.where(row < 4, row, LANES - 8 + row), 1.0, 0.0)
    edge = exact_dot(pick, orb[...].reshape(ORBS * ROWS, LANES), NT)
    zface[0] = edge[0:4]
    zface[1] = edge[4:8]

    pl.semaphore_wait(barrier, len(everyone))
    halos = [
        remote(orb.at[:, pl.ds(192, 64), :], xhalo.at[0], sendh.at[0], recvh.at[0], (1, 0, 0)),
        remote(orb.at[:, pl.ds(0, 64), :], xhalo.at[1], sendh.at[1], recvh.at[1], (-1, 0, 0)),
        remote(yface.at[1], yhalo.at[0], sendh.at[2], recvh.at[2], (0, 1, 0)),
        remote(yface.at[0], yhalo.at[1], sendh.at[3], recvh.at[3], (0, -1, 0)),
        remote(zface.at[1], zhalo.at[0], sendh.at[4], recvh.at[4], (0, 0, 1)),
        remote(zface.at[0], zhalo.at[1], sendh.at[5], recvh.at[5], (0, 0, -1)),
    ]
    for copy in halos:
        copy.start()
    everything = list(halos)

    loads[7].wait()
    gram[...] = jnp.zeros_like(gram)
    collect(1, 3, locked_rows)
    gstage[0, :, 0:64] = gram[0:32, :]
    gstage[0, :, 64:128] = gram[32:64, :]
    sent = reduce_start(gstage.at[0], gslots, sendg, recvg, 0, groups[0])
    everything += sent
    collect(3, STEPS)
    gtotal = reduce_finish(gstage[0], gslots, 0, sent)
    gstage[1] = gtotal
    base = len(groups[0])
    sent = reduce_start(gstage.at[1], gslots, sendg, recvg, base, groups[1])
    everything += sent

    for p in range(CHANNELS):
        sums[:, p, :] = (
            acc[p * OWNERS : (p + 1) * OWNERS, 0:NS]
            + acc[PAIR + p * OWNERS : PAIR + (p + 1) * OWNERS, 0:NS]
        )
    first = [
        remote(sums.at[c], landed.at[c], send1.at[c], recv1.at[c], offset_of(c)) for c in CODES
    ]
    for copy in first:
        copy.start()
    everything += first

    channel = ids((CHANNELS, NS), 0).astype(F32)
    copies = jnp.where(ids((SLOTS, NS), 1) % SLOTS == ids((SLOTS, NS), 0), 1.0, 0.0)
    grown = exact_dot(jnp.concatenate([strength[p] for p in range(CHANNELS)], axis=0), copies)
    limit = exact_dot(jnp.broadcast_to(chans[...], (8, SLOTS)).astype(F32), copies)[0:1]
    scale = jnp.where(channel < limit - 0.5, grown, 0.0)

    gtotal = reduce_finish(gtotal, gslots, base, sent)
    gstage[2] = gtotal
    base += len(groups[1])
    sent = reduce_start(gstage.at[2], gslots, sendg, recvg, base, groups[2])
    everything += sent

    loads[8].wait()
    for copy in halos:
        copy.wait_recv()
    ends[0:4] = zhalo[0]
    ends[4:8] = zhalo[1]
    square = (LANES, LANES)
    inner = by_distance(jnp.abs(ids(square, 0) - ids(square, 1)), -1.5 * STENCIL_WEIGHTS[0])
    place = jnp.where(row < 4, row - 4, LANES - 4 + row)
    outer = by_distance(jnp.abs(place - lane_id), 0.0)
    for n in range(ORBS):
        centre = orb[n]
        total = exact_dot(centre, inner)
        total += exact_dot(ends[:, n * ROWS : (n + 1) * ROWS], outer, TN)
        total += potential[...] * centre
        long = jnp.concatenate([xhalo[0, n], centre, xhalo[1, n]], axis=0)
        tall[:, 0:4, :] = yhalo[0, n * 16 : (n + 1) * 16]
        tall[:, 4:20, :] = centre.reshape(16, 16, LANES)
        tall[:, 20:24, :] = yhalo[1, n * 16 : (n + 1) * 16]
        for k in range(1, 5):
            pair = long[64 - 16 * k : 320 - 16 * k] + long[64 + 16 * k : 320 + 16 * k]
            side = tall[:, 4 - k : 20 - k, :] + tall[:, 4 + k : 20 + k, :]
            total += (-0.5 * STENCIL_WEIGHTS[k]) * (pair + side.reshape(ROWS, LANES))
        local[n] = total

    total = sums[13]
    for code, copy in zip(CODES, first):
        copy.wait_recv()
        total = total + landed[code]
    weighted[...] = total * scale
    second = []
    for code in CODES:
        opposite = tuple(-move for move in offset_of(code))
        copy = remote(weighted, returned.at[code], send2.at[code], recv2.at[code], opposite)
        copy.start()
        second.append(copy)
    returned[13] = weighted[...]
    everything += second

    packed = reduce_finish(gtotal, gslots, base, sent)
    matrix = jnp.concatenate([packed[:, 0:64], packed[:, 64:128]], axis=0)
    gram[...] = eliminate(matrix, 0, LOCKED)

    for copy in second:
        copy.wait_recv()
    stacked = [
        jnp.concatenate([returned[0:27, p, :], jnp.zeros((OWNERS - 27, NS), F32)], axis=0)
        for p in range(CHANNELS)
    ]
    high, rest = split(jnp.concatenate(stacked, axis=0).T)
    back[...] = jnp.concatenate([high, rest, high], axis=1)
    spread[...] = jnp.zeros_like(spread)

    def scatter(start, stop):
        @pl.loop(start, stop)
        def _(step):
            here = pl.ds(pl.multiple_of(step * CHUNK, CHUNK), CHUNK)
            lane, low, block = cell_parts(cell[:, here])
            hot = cell_onehot(lane, block)
            owners = onehot(OWNERS, owner[:, here])
            parts = [split(prof[p, :, here]) for p in range(CHANNELS)]
            most = spread_rows([part[0] for part in parts], owners)
            less = spread_rows([part[1] for part in parts], owners)
            near = jnp.dot(
                back[...], jnp.concatenate([most, most, less], axis=0), preferred_element_type=F32
            )
            hit = ids((SLOTS, CHUNK), 0) == atom[:, here]
            terms = picked_rows(near, hit, ORBS, SLOTS).astype(BF16)
            spread[...] += lax.dot_general(
                spread_rows(each_row(terms), onehot(RH, low)), hot, NT, preferred_element_type=F32
            )

    scatter(0, STEPS)

    for n in range(ORBS):
        for b in range(NB):
            applied[b * RH : (b + 1) * RH, n, :] = (
                local[n, b * RH : (b + 1) * RH, :]
                + spread[n * RH : (n + 1) * RH, b * LANES : (b + 1) * LANES]
            )
    value = jnp.zeros((ORBS, LOCKED), F32)
    for g in range(ROWS // 16):
        mine = jnp.concatenate([applied[g * 16 + r].astype(BF16) for r in range(16)], axis=1)
        kept = jnp.concatenate([lines[g * 16 + r] for r in range(16)], axis=1)
        value += lax.dot_general(mine, kept, NT, preferred_element_type=F32)
    value = jnp.concatenate([value, jnp.zeros((ORBS, 128 - LOCKED), F32)], axis=1)

    base = 0
    for level, group in enumerate(quick):
        cstage[level] = value
        csent = reduce_start(cstage.at[level], cslots, sendc, recvc, base, group)
        everything += csent
        value = reduce_finish(value, cslots, base, csent)
        base += len(group)

    mixing = exact_dot(value[:, 0:LOCKED], gram[...]).astype(BF16).astype(F32)
    aside = jnp.zeros((ORBS, LOCKED), F32)
    weights = jnp.concatenate(
        [
            jnp.concatenate([mixing if i == j else aside for i in range(4)], axis=1)
            for j in range(4)
        ],
        axis=0,
    ).astype(BF16)
    @pl.loop(0, 2)
    def _(step):
        for g in range(16):
            first_row = step * 128 + g * 8
            sides = [
                lines[pl.ds(first_row + 4 * h, 4)].reshape(4 * LOCKED, LANES) for h in range(2)
            ]
            fix = jnp.dot(weights, jnp.concatenate(sides, axis=1), preferred_element_type=F32)
            for h in range(2):
                for j in range(4):
                    r = first_row + 4 * h + j
                    out[:, r, :] = (
                        applied[r] - fix[j * ORBS : (j + 1) * ORBS, h * LANES : (h + 1) * LANES]
                    )

    for copy in everything:
        copy.wait_send()


def on_device(
    orbitals, potential, locked, sphere_cell, sphere_owner, sphere_atom,
    sphere_profile, atom_strength, atom_channels,
):
    dma = pltpu.SemaphoreType.DMA
    shapes = (
        ((ORBS, ROWS, LANES), F32), ((1, POINTS), jnp.int32), ((1, POINTS), jnp.int32),
        ((1, POINTS), jnp.int32), ((CHANNELS, 1, POINTS), F32), ((LOCKED, ROWS, LANES), BF16),
        ((CHANNELS, 1, SLOTS), F32), ((1, SLOTS), jnp.int32), ((ROWS, LANES), F32),
    )
    work = (
        ((ORBS * RH, NB * LANES), BF16), ((2 * PAIR, NS), F32), ((LOCKED * 32, LANES), F32),
        ((ROWS, LOCKED, LANES), BF16), ((2, ORBS * 16, 4, LANES), F32),
        ((2, 4, ORBS * ROWS), F32), ((OWNERS, CHANNELS, NS), F32), ((27, CHANNELS, NS), F32),
        ((CHANNELS, NS), F32), ((27, CHANNELS, NS), F32), ((2, ORBS, 64, LANES), F32),
        ((2, ORBS * 16, 4, LANES), F32), ((2, 4, ORBS * ROWS), F32), ((LOCKED, LOCKED), F32),
        ((3, 32, 128), F32), ((17, 32, 128), F32), ((NS, 3 * PAIR), BF16),
        ((ORBS, ROWS, LANES), F32), ((16, 24, LANES), F32), ((8, ORBS * ROWS), F32),
        ((ORBS * RH, NB * LANES), F32), ((ROWS, ORBS, LANES), F32), ((2, ORBS, 128), F32),
        ((30, ORBS, 128), F32),
    )
    out = pl.pallas_call(
        body,
        in_specs=[pl.BlockSpec(memory_space=pltpu.HBM)] * 9,
        out_specs=pl.BlockSpec(memory_space=pltpu.VMEM),
        out_shape=jax.ShapeDtypeStruct((ORBS, ROWS, LANES), F32),
        scratch_shapes=[pltpu.VMEM(*shape) for shape in shapes]
        + [dma((9,))]
        + [pltpu.VMEM(*shape) for shape in work]
        + [dma((count,)) for count in (27, 27, 27, 27, 17, 17, 6, 6, 30, 30)],
        compiler_params=pltpu.CompilerParams(
            collective_id=0, has_side_effects=True, vmem_limit_bytes=44 << 20
        ),
        name="apply_and_project",
    )(*(pltpu.with_memory_space_constraint(array, pltpu.HBM) for array in (
        orbitals.reshape(ORBS, ROWS, LANES),
        sphere_cell.reshape(1, POINTS),
        sphere_owner.reshape(1, POINTS),
        sphere_atom.reshape(1, POINTS),
        sphere_profile.reshape(CHANNELS, 1, POINTS),
        locked.reshape(LOCKED, ROWS, LANES),
        jnp.transpose(atom_strength, (0, 1, 4, 2, 3)).reshape(CHANNELS, 1, SLOTS),
        atom_channels.reshape(1, SLOTS),
        potential.reshape(ROWS, LANES),
    )))
    return out.reshape(orbitals.shape)


def solution(mesh):
    placed = (
        P(None, "gx", "gy", "gz"),
        P("gx", "gy", "gz"),
        P(None, "gx", "gy", "gz"),
        P("gx", "gy", "gz", None),
        P("gx", "gy", "gz", None),
        P("gx", "gy", "gz", None),
        P("gx", "gy", "gz", None, None),
        P("gx", "gy", "gz", None, None),
        P("gx", "gy", "gz", None),
    )
    return jax.shard_map(
        on_device, mesh=mesh, in_specs=placed, out_specs=P(None, "gx", "gy", "gz"), check_vma=False
    )
```

```python
import jax
import jax.numpy as jnp
import numpy as np
from jax import lax
from jax.experimental import pallas as pl
from jax.experimental.pallas import tpu as pltpu
from jax.sharding import PartitionSpec as P

STENCIL_WEIGHTS = (-205.0 / 72.0, 8.0 / 5.0, -1.0 / 5.0, 8.0 / 315.0, -1.0 / 560.0)
MESH = pl.DeviceIdType.MESH
F32 = jnp.float32
BF16 = jnp.bfloat16
HIGHEST = lax.Precision.HIGHEST

ORBS = 8
ROWS = 256
LANES = 128
SLOTS = 32
OWNERS = 32
CHANNELS = 9
POINTS = 16384
LOCKED = 64
CHUNK = 4096
STEPS = POINTS // CHUNK
RH = 32
NB = ROWS // RH
PAIR = CHANNELS * OWNERS
NS = ORBS * SLOTS

NT = (((1,), (1,)), ((), ()))
TN = (((0,), (0,)), ((), ()))


def onehot(count, index):
    ids = lax.broadcasted_iota(jnp.int32, (count, index.shape[1]), 0)
    return jnp.where(ids == index, 1.0, 0.0).astype(BF16)


def cell_parts(cell):
    line = cell >> 7
    return cell & (LANES - 1), line & (RH - 1), line // RH


def cell_onehot(lane, block):
    lanes = onehot(LANES, lane)
    blocks = onehot(16, block)
    return jnp.concatenate([lanes * blocks[b : b + 1] for b in range(NB)], axis=0)


def split(value):
    high = value.astype(BF16)
    return high, (value - high.astype(F32)).astype(BF16)


def spread_rows(rows, mask):
    return jnp.concatenate([mask * row for row in rows], axis=0)


def each_row(value):
    return [value[i : i + 1] for i in range(value.shape[0])]


def picked_rows(values, hit, count, height):
    parts = [
        jnp.sum(jnp.where(hit, values[n * height : (n + 1) * height], 0.0), axis=0, keepdims=True)
        for n in range(count)
    ]
    return jnp.concatenate(parts, axis=0)


def offset_of(code):
    return code // 9 - 1, code // 3 % 3 - 1, code % 3 - 1


CODES = sorted(
    (code for code in range(27) if code != 13),
    key=lambda code: -sum(abs(move) for move in offset_of(code)),
)


def device(shift):
    spot = []
    for name, move in zip(("gx", "gy", "gz"), shift):
        size, mine = lax.axis_size(name), lax.axis_index(name)
        if move == "flip":
            spot.append(mine + 1 - 2 * lax.rem(mine, 2))
        else:
            spot.append(lax.rem(mine + move % size, size))
    return tuple(spot)


def quick_partners():
    one, two = [], []
    for k in range(lax.axis_size("gz")):
        one += [(0, 0, k), ("flip", 0, k)]
    for k in range(lax.axis_size("gy")):
        two += [(0, k, 0), (lax.axis_size("gx") // 2, k, 0)]
    return one[1:], two[1:]


def axis_partners():
    found = []
    for axis, name in ((2, "gz"), (1, "gy"), (0, "gx")):
        group = []
        for k in range(1, lax.axis_size(name)):
            shift = [0, 0, 0]
            shift[axis] = k
            group.append(tuple(shift))
        found.append(group)
    return found


def canonical(shift):
    sizes = [lax.axis_size(name) for name in ("gx", "gy", "gz")]
    return tuple(move if move == "flip" else move % size for move, size in zip(shift, sizes))


def remote(source, target, send, receive, shift):
    return pltpu.make_async_remote_copy(
        src_ref=source, dst_ref=target, send_sem=send, recv_sem=receive,
        device_id=device(shift), device_id_type=MESH,
    )


def reduce_start(source, slots, send, receive, base, group):
    copies = [
        remote(source, slots.at[base + k], send.at[base + k], receive.at[base + k], shift)
        for k, shift in enumerate(group)
    ]
    for copy in copies:
        copy.start()
    return copies


def reduce_finish(own, slots, base, copies):
    total = own
    for k, copy in enumerate(copies):
        copy.wait_recv()
        total = total + slots[base + k]
    return total


def ids(shape, dimension):
    return lax.broadcasted_iota(jnp.int32, shape, dimension)


def by_distance(distance, centre):
    total = jnp.where(distance == 0, centre, 0.0)
    for k in range(1, 5):
        total = jnp.where(distance == k, -0.5 * STENCIL_WEIGHTS[k], total)
    return total


def exact_dot(left, right, dims=(((1,), (0,)), ((), ()))):
    return lax.dot_general(left, right, dims, precision=HIGHEST, preferred_element_type=F32)


def eliminate(matrix, start, stop):
    columns, rows = ids(matrix.shape, 1), ids(matrix.shape, 0)
    for k in range(start, stop):
        scale = 1.0 / matrix[k : k + 1, k : k + 1]
        column = matrix[:, k : k + 1]
        cleared = jnp.where(columns == k, jnp.where(rows == k, 1.0, 0.0), matrix)
        line = cleared[k : k + 1, :] * scale
        matrix = jnp.where(rows == k, line, cleared - column * line)
    return matrix


def body(
    orb_h, cell_h, owner_h, atom_h, prof_h, locked_h, strength_h, chans_h, potential_h,
    out,
    orb, cell, owner, atom, prof, locked, strength, chans, potential, arrived,
    table, acc, wide, lines, yface, zface, sums, landed, weighted, returned,
    xhalo, yhalo, zhalo, gram, gstage, gslots, back, local, tall, ends, spread, applied,
    cstage, cslots,
    send1, recv1, send2, recv2, sendg, recvg, sendh, recvh, sendc, recvc,
):
    groups = axis_partners()
    everyone = {canonical(offset_of(code)) for code in CODES}
    quick = quick_partners()
    for group in groups + list(quick):
        everyone |= {canonical(shift) for shift in group}
    near = {0, 1, lax.axis_size("gz") - 1}
    everyone = [shift for shift in everyone if shift[0] != "flip" or shift[2] not in near]
    everyone = sorted(everyone, key=str)
    loads = [
        pltpu.make_async_copy(source, target, arrived.at[k])
        for k, (source, target) in enumerate(
            (
                (orb_h, orb), (cell_h, cell), (owner_h, owner), (atom_h, atom), (prof_h, prof),
                (strength_h, strength), (chans_h, chans), (locked_h, locked),
                (potential_h, potential),
            )
        )
    ]
    for load in loads:
        load.start()
    barrier = pltpu.get_barrier_semaphore()
    for shift in everyone:
        pl.semaphore_signal(barrier, inc=1, device_id=device(shift), device_id_type=MESH)
    loads[0].wait()

    for n in range(ORBS):
        for b in range(NB):
            table[n * RH : (n + 1) * RH, b * LANES : (b + 1) * LANES] = orb[
                n, b * RH : (b + 1) * RH, :
            ].astype(BF16)
    for load in loads[1:7]:
        load.wait()
    acc[...] = jnp.zeros_like(acc)

    def collect(start, stop):
        @pl.loop(start, stop)
        def _(step):
            here = pl.ds(pl.multiple_of(step * CHUNK, CHUNK), CHUNK)
            lane, low, block = cell_parts(cell[:, here])
            found = jnp.dot(table[...], cell_onehot(lane, block), preferred_element_type=F32)
            values = picked_rows(found, ids((RH, CHUNK), 0) == low, ORBS, RH).astype(BF16)
            right = spread_rows(each_row(values), onehot(SLOTS, atom[:, here]))
            owners = onehot(OWNERS, owner[:, here])
            parts = [split(prof[p, :, here]) for p in range(CHANNELS)]
            left = jnp.concatenate(
                [spread_rows([part[k] for part in parts], owners) for k in range(2)], axis=0
            )
            acc[0 : 2 * PAIR, 0:NS] += lax.dot_general(left, right, NT, preferred_element_type=F32)

    def locked_rows(step):
        for part in range(8):
            here = pl.ds(pl.multiple_of(step * 128 + part * 16, 16), 16)
            room = wide.at[pl.ds((part % 2) * 1024, 1024)]
            room[...] = locked[:, here, :].astype(F32).reshape(LOCKED * 16, LANES)
            rows = [room[pl.ds(r, LOCKED, stride=16), :].astype(BF16) for r in range(16)]
            for r in range(16):
                lines[step * 128 + part * 16 + r] = rows[r]
            flat = jnp.concatenate(rows, axis=1)
            gram[...] += lax.dot_general(flat, flat, NT, preferred_element_type=F32)

    collect(0, 1)
    whole = orb[...].reshape(ORBS * 16, 16, LANES)
    yface[0] = whole[:, 0:4, :]
    yface[1] = whole[:, 12:16, :]
    row, lane_id = ids((8, LANES), 0), ids((8, LANES), 1)
    pick = jnp.where(lane_id == jnp.where(row < 4, row, LANES - 8 + row), 1.0, 0.0)
    edge = exact_dot(pick, orb[...].reshape(ORBS * ROWS, LANES), NT)
    zface[0] = edge[0:4]
    zface[1] = edge[4:8]

    pl.semaphore_wait(barrier, len(everyone))
    halos = [
        remote(orb.at[:, pl.ds(192, 64), :], xhalo.at[0], sendh.at[0], recvh.at[0], (1, 0, 0)),
        remote(orb.at[:, pl.ds(0, 64), :], xhalo.at[1], sendh.at[1], recvh.at[1], (-1, 0, 0)),
        remote(yface.at[1], yhalo.at[0], sendh.at[2], recvh.at[2], (0, 1, 0)),
        remote(yface.at[0], yhalo.at[1], sendh.at[3], recvh.at[3], (0, -1, 0)),
        remote(zface.at[1], zhalo.at[0], sendh.at[4], recvh.at[4], (0, 0, 1)),
        remote(zface.at[0], zhalo.at[1], sendh.at[5], recvh.at[5], (0, 0, -1)),
    ]
    for copy in halos:
        copy.start()
    everything = list(halos)

    collect(1, STEPS)
    for p in range(CHANNELS):
        sums[:, p, :] = (
            acc[p * OWNERS : (p + 1) * OWNERS, 0:NS]
            + acc[PAIR + p * OWNERS : PAIR + (p + 1) * OWNERS, 0:NS]
        )
    first = [
        remote(sums.at[c], landed.at[c], send1.at[c], recv1.at[c], offset_of(c)) for c in CODES
    ]
    for copy in first:
        copy.start()
    everything += first

    loads[7].wait()
    gram[...] = jnp.zeros_like(gram)
    pl.loop(0, 2)(locked_rows)
    gstage[0, :, 0:64] = gram[0:32, :]
    gstage[0, :, 64:128] = gram[32:64, :]
    sent = reduce_start(gstage.at[0], gslots, sendg, recvg, 0, groups[0])
    everything += sent

    channel = ids((CHANNELS, NS), 0).astype(F32)
    copies = jnp.where(ids((SLOTS, NS), 1) % SLOTS == ids((SLOTS, NS), 0), 1.0, 0.0)
    grown = exact_dot(jnp.concatenate([strength[p] for p in range(CHANNELS)], axis=0), copies)
    limit = exact_dot(jnp.broadcast_to(chans[...], (8, SLOTS)).astype(F32), copies)[0:1]
    scale = jnp.where(channel < limit - 0.5, grown, 0.0)

    total = sums[13]
    for code, copy in zip(CODES, first):
        copy.wait_recv()
        total = total + landed[code]
    weighted[...] = total * scale
    second = []
    for code in CODES:
        opposite = tuple(-move for move in offset_of(code))
        copy = remote(weighted, returned.at[code], send2.at[code], recv2.at[code], opposite)
        copy.start()
        second.append(copy)
    returned[13] = weighted[...]
    everything += second

    gtotal = reduce_finish(gstage[0], gslots, 0, sent)
    gstage[1] = gtotal
    middle = len(groups[0])
    sent = reduce_start(gstage.at[1], gslots, sendg, recvg, middle, groups[1])
    everything += sent

    loads[8].wait()
    for copy in halos:
        copy.wait_recv()
    ends[0:4] = zhalo[0]
    ends[4:8] = zhalo[1]
    square = (LANES, LANES)
    inner = by_distance(jnp.abs(ids(square, 0) - ids(square, 1)), -1.5 * STENCIL_WEIGHTS[0])
    place = jnp.where(row < 4, row - 4, LANES - 4 + row)
    outer = by_distance(jnp.abs(place - lane_id), 0.0)
    for n in range(ORBS):
        centre = orb[n]
        total = exact_dot(centre, inner)
        total += exact_dot(ends[:, n * ROWS : (n + 1) * ROWS], outer, TN)
        total += potential[...] * centre
        long = jnp.concatenate([xhalo[0, n], centre, xhalo[1, n]], axis=0)
        tall[:, 0:4, :] = yhalo[0, n * 16 : (n + 1) * 16]
        tall[:, 4:20, :] = centre.reshape(16, 16, LANES)
        tall[:, 20:24, :] = yhalo[1, n * 16 : (n + 1) * 16]
        for k in range(1, 5):
            pair = long[64 - 16 * k : 320 - 16 * k] + long[64 + 16 * k : 320 + 16 * k]
            side = tall[:, 4 - k : 20 - k, :] + tall[:, 4 + k : 20 + k, :]
            total += (-0.5 * STENCIL_WEIGHTS[k]) * (pair + side.reshape(ROWS, LANES))
        local[n] = total

    for copy in second:
        copy.wait_recv()
    stacked = [
        jnp.concatenate([returned[0:27, p, :], jnp.zeros((OWNERS - 27, NS), F32)], axis=0)
        for p in range(CHANNELS)
    ]
    high, rest = split(jnp.concatenate(stacked, axis=0).T)
    back[...] = jnp.concatenate([high, rest, high], axis=1)
    spread[...] = jnp.zeros_like(spread)

    def scatter(start, stop):
        @pl.loop(start, stop)
        def _(step):
            here = pl.ds(pl.multiple_of(step * CHUNK, CHUNK), CHUNK)
            lane, low, block = cell_parts(cell[:, here])
            hot = cell_onehot(lane, block)
            owners = onehot(OWNERS, owner[:, here])
            parts = [split(prof[p, :, here]) for p in range(CHANNELS)]
            most = spread_rows([part[0] for part in parts], owners)
            less = spread_rows([part[1] for part in parts], owners)
            near = jnp.dot(
                back[...], jnp.concatenate([most, most, less], axis=0), preferred_element_type=F32
            )
            hit = ids((SLOTS, CHUNK), 0) == atom[:, here]
            terms = picked_rows(near, hit, ORBS, SLOTS).astype(BF16)
            spread[...] += lax.dot_general(
                spread_rows(each_row(terms), onehot(RH, low)), hot, NT, preferred_element_type=F32
            )

    scatter(0, STEPS // 2)
    gtotal = reduce_finish(gtotal, gslots, middle, sent)
    gstage[2] = gtotal
    middle += len(groups[1])
    sent = reduce_start(gstage.at[2], gslots, sendg, recvg, middle, groups[2])
    everything += sent
    scatter(STEPS // 2, STEPS)

    for n in range(ORBS):
        for b in range(NB):
            applied[b * RH : (b + 1) * RH, n, :] = (
                local[n, b * RH : (b + 1) * RH, :]
                + spread[n * RH : (n + 1) * RH, b * LANES : (b + 1) * LANES]
            )
    value = jnp.zeros((ORBS, LOCKED), F32)
    for g in range(ROWS // 16):
        mine = jnp.concatenate([applied[g * 16 + r].astype(BF16) for r in range(16)], axis=1)
        kept = jnp.concatenate([lines[g * 16 + r] for r in range(16)], axis=1)
        value += lax.dot_general(mine, kept, NT, preferred_element_type=F32)
    value = jnp.concatenate([value, jnp.zeros((ORBS, 128 - LOCKED), F32)], axis=1)

    base = 0
    for level, group in enumerate(quick):
        cstage[level] = value
        csent = reduce_start(cstage.at[level], cslots, sendc, recvc, base, group)
        everything += csent
        if level == 0:
            packed = reduce_finish(gtotal, gslots, middle, sent)
            matrix = jnp.concatenate([packed[:, 0:64], packed[:, 64:128]], axis=0)
        matrix = eliminate(matrix, level * 32, level * 32 + 32)
        value = reduce_finish(value, cslots, base, csent)
        base += len(group)

    mixing = exact_dot(value[:, 0:LOCKED], matrix).astype(BF16).astype(F32)
    aside = jnp.zeros((ORBS, LOCKED), F32)
    weights = jnp.concatenate(
        [
            jnp.concatenate([mixing if i == j else aside for i in range(4)], axis=1)
            for j in range(4)
        ],
        axis=0,
    ).astype(BF16)
    @pl.loop(0, 2)
    def _(step):
        for g in range(16):
            first_row = step * 128 + g * 8
            sides = [
                lines[pl.ds(first_row + 4 * h, 4)].reshape(4 * LOCKED, LANES) for h in range(2)
            ]
            fix = jnp.dot(weights, jnp.concatenate(sides, axis=1), preferred_element_type=F32)
            for h in range(2):
                for j in range(4):
                    r = first_row + 4 * h + j
                    out[:, r, :] = (
                        applied[r] - fix[j * ORBS : (j + 1) * ORBS, h * LANES : (h + 1) * LANES]
                    )

    for copy in everything:
        copy.wait_send()


def on_device(
    orbitals, potential, locked, sphere_cell, sphere_owner, sphere_atom,
    sphere_profile, atom_strength, atom_channels,
):
    dma = pltpu.SemaphoreType.DMA
    shapes = (
        ((ORBS, ROWS, LANES), F32), ((1, POINTS), jnp.int32), ((1, POINTS), jnp.int32),
        ((1, POINTS), jnp.int32), ((CHANNELS, 1, POINTS), F32), ((LOCKED, ROWS, LANES), BF16),
        ((CHANNELS, 1, SLOTS), F32), ((1, SLOTS), jnp.int32), ((ROWS, LANES), F32),
    )
    work = (
        ((ORBS * RH, NB * LANES), BF16), ((2 * PAIR, NS), F32), ((LOCKED * 32, LANES), F32),
        ((ROWS, LOCKED, LANES), BF16), ((2, ORBS * 16, 4, LANES), F32),
        ((2, 4, ORBS * ROWS), F32), ((OWNERS, CHANNELS, NS), F32), ((27, CHANNELS, NS), F32),
        ((CHANNELS, NS), F32), ((27, CHANNELS, NS), F32), ((2, ORBS, 64, LANES), F32),
        ((2, ORBS * 16, 4, LANES), F32), ((2, 4, ORBS * ROWS), F32), ((LOCKED, LOCKED), F32),
        ((3, 32, 128), F32), ((17, 32, 128), F32), ((NS, 3 * PAIR), BF16),
        ((ORBS, ROWS, LANES), F32), ((16, 24, LANES), F32), ((8, ORBS * ROWS), F32),
        ((ORBS * RH, NB * LANES), F32), ((ROWS, ORBS, LANES), F32), ((2, ORBS, 128), F32),
        ((30, ORBS, 128), F32),
    )
    out = pl.pallas_call(
        body,
        in_specs=[pl.BlockSpec(memory_space=pltpu.HBM)] * 9,
        out_specs=pl.BlockSpec(memory_space=pltpu.VMEM),
        out_shape=jax.ShapeDtypeStruct((ORBS, ROWS, LANES), F32),
        scratch_shapes=[pltpu.VMEM(*shape) for shape in shapes]
        + [dma((9,))]
        + [pltpu.VMEM(*shape) for shape in work]
        + [dma((count,)) for count in (27, 27, 27, 27, 17, 17, 6, 6, 30, 30)],
        compiler_params=pltpu.CompilerParams(
            collective_id=0, has_side_effects=True, vmem_limit_bytes=44 << 20
        ),
        name="apply_and_project",
    )(*(pltpu.with_memory_space_constraint(array, pltpu.HBM) for array in (
        orbitals.reshape(ORBS, ROWS, LANES),
        sphere_cell.reshape(1, POINTS),
        sphere_owner.reshape(1, POINTS),
        sphere_atom.reshape(1, POINTS),
        sphere_profile.reshape(CHANNELS, 1, POINTS),
        locked.reshape(LOCKED, ROWS, LANES),
        jnp.transpose(atom_strength, (0, 1, 4, 2, 3)).reshape(CHANNELS, 1, SLOTS),
        atom_channels.reshape(1, SLOTS),
        potential.reshape(ROWS, LANES),
    )))
    return out.reshape(orbitals.shape)


def solution(mesh):
    placed = (
        P(None, "gx", "gy", "gz"),
        P("gx", "gy", "gz"),
        P(None, "gx", "gy", "gz"),
        P("gx", "gy", "gz", None),
        P("gx", "gy", "gz", None),
        P("gx", "gy", "gz", None),
        P("gx", "gy", "gz", None, None),
        P("gx", "gy", "gz", None, None),
        P("gx", "gy", "gz", None),
    )
    return jax.shard_map(
        on_device, mesh=mesh, in_specs=placed, out_specs=P(None, "gx", "gy", "gz"), check_vma=False
    )
```
